256 devices in a mesh: row: 16 (over z, y_lo), col: 16 (over y_hi, x, core).
Axes of the slice: x: 4, y: 4 (y_hi: 2, y_lo: 2; y = y_hi * 2 + y_lo), z: 8, core: 2. Of those that a mesh axis runs over, the one named last changes fastest.
Arguments:
- core_blocks: float32 [64, 2048, 128], P('row', 'col'), may hold values from -6 to 6
- block_coords: int32 [64, 32], replicated, may hold values from 0 to 9, as said below
- band_vectors: float32 [16, 16, 128], P('col'), may hold values from -6 to 6
- band_blocks: int32 [16, 16], P('col'), may hold values from 0 to 159, as said below
- spread: float32 [], replicated, may hold values from 12 to 24
Outputs:
- purified: float32 [64, 2048, 128], P('row', 'col')
The draws below stay inside these ranges and needn't reach their ends.
Inputs may be any that keep to these rules, and one draw needn't show every extreme that they name: `block_coords`: the first entry of a slot is a local block row below 10, the second a local block column below 10; the 4 slots of one tile name distinct blocks. `band_blocks`: the 16 block rows of one band are distinct.
All inputs are finite; a program needn't handle non-finite values.
Results may differ from the reference program's by a relative error of at most 0.0003.
Values sent between devices are 32-bit elements; how exact they have to be, the bound alone decides.
A program may use at most 64 MiB of HBM per device.

```python
import math
import jax
import jax.numpy as jnp
from jax import lax

BS = 128
NB = 160
SLOTS = 4
BANDS = 16
SUPPORT = 16
LBR = 10
LBC = 10
M_RATIO = 1
N_ROW = 16
N_COL = 16


def pick_positions(one_key):
    return jax.random.permutation(one_key, 2 * LBC)[:SLOTS]


def pick_blocks(one_key):
    return jax.random.permutation(one_key, NB)[:SUPPORT]


def draw_block_coords(key, part):
    keys = jax.random.split(key, N_ROW * N_COL)
    picks = jax.vmap(pick_positions)(keys).astype(jnp.int32)
    corner = LBC - 1
    first = picks[0]
    present = jnp.any(first == corner)
    first = first.at[0].set(jnp.where(present, first[0], corner))
    picks = picks.at[0].set(first)
    offset = picks // LBC
    within_tile = picks % LBC
    piece = within_tile // LBR
    local_row = within_tile % LBR
    local_col = piece * LBR + (local_row + offset) % LBR
    coords = jnp.stack([local_row, local_col], axis=-1).astype(jnp.int32)
    coords = coords.reshape(N_ROW, N_COL, SLOTS, 2).transpose(0, 2, 1, 3)
    return coords.reshape(N_ROW * SLOTS, N_COL * 2)


def draw_band_blocks(key, part):
    keys = jax.random.split(key, BANDS)
    picks = jax.vmap(pick_blocks)(keys).astype(jnp.int32)
    corner = NB - 1
    first = picks[0]
    present = jnp.any(first == corner)
    first = first.at[0].set(jnp.where(present, first[0], corner))
    return picks.at[0].set(first)


def levels(rng, shape, pieces, smallest, top_value):
    loudness = 1.0
    for axis_at, blocks in pieces:
        heights = jax.random.uniform(jax.random.fold_in(jax.random.fold_in(rng, 6), axis_at), (blocks,), jnp.float32, smallest / len(pieces), top_value / len(pieces))
        loudness = loudness * jnp.repeat(jnp.exp(heights), shape[axis_at] // blocks).reshape((-1,) + (1,) * (len(shape) - 1 - axis_at))
    return loudness


def normal_values(stream_key, shape, deviation, limit, cuts=(), held_as=jnp.bfloat16):
    factor_of = levels(stream_key, shape, cuts, -0.22, 0.18) if cuts else 1.0
    drawn = jax.random.normal(stream_key, shape, jnp.float32) * deviation * factor_of
    return jnp.minimum(jnp.maximum(drawn, -limit), limit).astype(held_as)


def setup_inputs(seed: int = 0) -> dict:
    seeds = jax.random.split(jax.random.key(seed), 6)
    return {
        "core_blocks": normal_values(seeds[0], (N_ROW * SLOTS, N_COL * BS, BS), 1.0, 6.0, ((0, 16), (1, 16)), jnp.float32),
        "block_coords": draw_block_coords(jax.random.fold_in(seeds[5], 71), 0),
        "band_vectors": normal_values(seeds[2], (BANDS, SUPPORT, BS), 1.0, 6.0, ((0, 16),), jnp.float32),
        "band_blocks": draw_band_blocks(jax.random.fold_in(seeds[5], 71), 0),
        "spread": jnp.clip(jnp.exp(jax.random.uniform(seeds[4], (), jnp.float32, math.log(12.0), math.log(24.0))), 12.0, 24.0),
    }


highest = lax.Precision.HIGHEST


def to_tiles(blocks):
    return blocks.reshape(N_ROW, SLOTS, N_COL, BS, BS).transpose(0, 2, 1, 3, 4)


def from_tiles(tiles):
    return tiles.transpose(0, 2, 1, 3, 4).reshape(N_ROW * SLOTS, N_COL * BS, BS)


def tile_pattern(block_coords):
    local = block_coords.reshape(N_ROW, SLOTS, N_COL, 2).transpose(0, 2, 1, 3)
    tile_row = jnp.arange(N_ROW, dtype=jnp.int32)[:, None, None]
    tile_col = jnp.arange(N_COL, dtype=jnp.int32)[None, :, None]
    global_rows = tile_row * LBR + local[:, :, :, 0]
    global_cols = tile_col * LBC + local[:, :, :, 1]
    return local, global_rows, global_cols


def exchange_part(band_vectors, band_blocks, global_rows, global_cols):
    hit_row = (band_blocks[:, :, None, None, None] == global_rows[None, None]).astype(jnp.float32)
    hit_col = (band_blocks[:, :, None, None, None] == global_cols[None, None]).astype(jnp.float32)
    vec_row = jnp.einsum('blrcs,blx->brcsx', hit_row, band_vectors, precision=highest)
    vec_col = jnp.einsum('blrcs,blx->brcsx', hit_col, band_vectors, precision=highest)
    return -jnp.einsum('brcsx,brcsy->rcsxy', vec_row, vec_col, precision=highest)


def link_weights(targets, left_local, piece, right_local):
    row_target = targets[:, :, None, None, 0]
    col_target = targets[:, :, None, None, 1]
    row_left = left_local[None, None, :, None, 0]
    col_left = left_local[None, None, :, None, 1]
    row_right = right_local[:, None, None, :, 0]
    col_right = right_local[:, None, None, :, 1]
    keep = (row_left == row_target) & (col_left // LBR == piece)
    keep = keep & (col_left % LBR == row_right) & (col_right == col_target)
    return keep.astype(jnp.float32)


def product(left, right, local):
    def one_row(row_index):
        left_row = left[row_index]
        targets = local[row_index]

        def step(total, source):
            left_tile = lax.dynamic_index_in_dim(left_row, source // M_RATIO, 0, keepdims=False)
            left_local = lax.dynamic_index_in_dim(targets, source // M_RATIO, 0, keepdims=False)
            right_tiles = lax.dynamic_index_in_dim(right, source, 0, keepdims=False)
            right_local = lax.dynamic_index_in_dim(local, source, 0, keepdims=False)
            weight = link_weights(targets, left_local, source % M_RATIO, right_local)
            pairs = jnp.einsum('axk,cbky->caxby', left_tile, right_tiles, precision=highest)
            return total + jnp.einsum('ctab,caxby->ctxy', weight, pairs, precision=highest), None

        start = jnp.zeros((N_COL, SLOTS, BS, BS), jnp.float32)
        total, _ = lax.scan(step, start, jnp.arange(N_ROW, dtype=jnp.int32))
        return total

    return lax.map(one_row, jnp.arange(N_ROW, dtype=jnp.int32))


def reference(core_blocks, block_coords, band_vectors, band_blocks, spread):
    local, global_rows, global_cols = tile_pattern(block_coords)
    fock = to_tiles(core_blocks) + exchange_part(band_vectors, band_blocks, global_rows, global_cols)
    scaled = fock / spread
    square = product(scaled, scaled, local)
    cube = product(square, scaled, local)
    return from_tiles(1.5 * fock - 2.0 * spread * cube)
```

```python
import functools

import jax
import jax.numpy as jnp
from jax import lax
from jax.experimental import pallas as pl
from jax.experimental.pallas import tpu as pltpu
from jax.sharding import PartitionSpec as P

NB = 160
BS = 128
SLOTS = 4
MESH = pl.DeviceIdType.MESH

NZ = 8
NX = 4
HALF = 32
PACK = 12
TRIPLES = 20

highest = lax.Precision.HIGHEST


def shifted(block, axis, distance):
    devices = range(lax.axis_size(axis))
    route = [((i - distance) % len(devices), i) for i in devices]
    return lax.ppermute(block, axis, route)


def exchange_term(vectors, blocks, block_rows, block_cols):
    hit_row = (blocks[:, :, None] == block_rows[None, None, :]).astype(jnp.float32)
    hit_col = (blocks[:, :, None] == block_cols[None, None, :]).astype(jnp.float32)
    vec_row = jnp.einsum("bln,blx->bnx", hit_row, vectors, precision=highest)
    vec_col = jnp.einsum("bln,blx->bnx", hit_col, vectors, precision=highest)
    return -jnp.einsum("bnx,bny->nxy", vec_row, vec_col, precision=highest)


def tile_layout(layout, tile_row, tile_col):
    slots = layout.shape[1]
    start = (tile_row, jnp.int32(0), tile_col, jnp.int32(0))
    return lax.dynamic_slice(layout, start, (1, slots, 1, 2)).reshape(slots, 2)


def link_weights(targets, left_local, piece, right_local, tile_rows):
    row_target = targets[:, None, None, 0]
    col_target = targets[:, None, None, 1]
    row_left = left_local[None, :, None, 0]
    col_left = left_local[None, :, None, 1]
    row_right = right_local[None, None, :, 0]
    col_right = right_local[None, None, :, 1]
    keep = (row_left == row_target) & (col_left // tile_rows == piece)
    keep = keep & (col_left % tile_rows == row_right) & (col_right == col_target)
    return keep.astype(jnp.float32)


def accumulate(
    total, targets, left_blocks, left_local, piece, right_blocks, right_local, tile_rows
):
    weight = link_weights(targets, left_local, piece, right_local, tile_rows)
    pairs = jnp.einsum("axk,bky->axby", left_blocks, right_blocks, precision=highest)
    return total + jnp.einsum("tab,axby->txy", weight, pairs, precision=highest)


def align(block, axis, amount):
    for place in range((lax.axis_size(axis) - 1).bit_length()):
        moved = shifted(block, axis, -(1 << place))
        block = jnp.where(amount >> place & 1 == 1, moved, block)
    return block


def shifted_product(left, right, layout, targets, this_row, this_col, tile_rows):
    row_count = lax.axis_size("row")
    left = align(left, "col", this_row)

    def step_body(step, carry):
        total, left, right = carry
        source = (this_row + this_col + step) % row_count
        left_local = tile_layout(layout, this_row, source)
        right_local = tile_layout(layout, source, this_col)
        total = accumulate(
            total, targets, left, left_local, 0, right, right_local, tile_rows
        )
        left = shifted(left, "col", -1)
        right = shifted(right, "row", -1)
        return (total, left, right)

    total, left, right = lax.fori_loop(
        0, row_count, step_body, (jnp.zeros_like(left), left, right)
    )
    return (total, right)


def general(core_blocks, block_coords, band_vectors, band_blocks, spread):
    row_count = lax.axis_size("row")
    column_count = lax.axis_size("col")
    tile_rows = NB // row_count
    tile_columns = NB // column_count
    slots = core_blocks.shape[0]
    this_row = lax.axis_index("row")
    this_col = lax.axis_index("col")
    layout = block_coords.reshape(row_count, slots, column_count, 2)
    targets = tile_layout(layout, this_row, this_col)
    vectors, blocks = (
        lax.all_gather(band_vectors, "col", axis=0, tiled=True),
        lax.all_gather(band_blocks, "col", axis=0, tiled=True),
    )
    block_rows = this_row * tile_rows + targets[:, 0]
    block_cols = this_col * tile_columns + targets[:, 1]
    exchange = exchange_term(vectors, blocks, block_rows, block_cols)
    fock = core_blocks + exchange
    scaled = fock / spread
    right = align(scaled, "row", this_col)
    square, right = shifted_product(
        scaled, right, layout, targets, this_row, this_col, tile_rows
    )
    cube, right = shifted_product(
        square, right, layout, targets, this_row, this_col, tile_rows
    )
    return 1.5 * fock - 2.0 * spread * cube


def fits(layout):
    n = layout.shape[0]
    tile = NB // n
    place = jnp.arange(NB, dtype=jnp.int32)
    grid = layout.transpose(1, 3, 0, 2)
    rows = jnp.repeat(jnp.repeat(grid[:, 0], tile, 1), tile, 2)
    cols = jnp.repeat(jnp.repeat(grid[:, 1], tile, 1), tile, 2)
    here = (rows == (place % tile)[None, :, None]) & (cols == (place % tile)[None, None, :])
    pattern = jnp.any(here, 0).astype(jnp.float32)
    spread_out = (place[:, None] // tile == jnp.arange(n)[None, :]).astype(jnp.float32)

    def per_tile(side):
        mask = (side == 1).astype(jnp.float32)
        links = pattern * jnp.dot(pattern * mask[None, :], pattern)
        return jnp.dot(spread_out.T, jnp.dot(links, spread_out))

    tiles = place // tile
    right_one = per_tile(tiles % 2)
    left_one = per_tile(tiles // 8)
    total = per_tile(jnp.ones_like(place))
    index = jnp.arange(n, dtype=jnp.int32)
    right_far = jnp.where((index % 2 == 1)[:, None], total - right_one, right_one)
    left_far = jnp.where((index // 8 == 1)[None, :], total - left_one, left_one)
    worst = jnp.maximum(jnp.max(right_far), jnp.max(left_far))
    return (worst <= PACK) & (jnp.max(total) <= TRIPLES)


def plan_of(layout, this_row, this_col):
    n = layout.shape[0]
    tile = NB // n
    k = jnp.arange(n, dtype=jnp.int32)

    def links(row, col):
        left = lax.dynamic_index_in_dim(layout, row, 0, False).transpose(1, 0, 2)
        right = lax.dynamic_index_in_dim(layout, col, 2, False)
        target = lax.dynamic_index_in_dim(left, col, 0, False)
        hit = (left[:, :, None, None, 0] == target[None, None, None, :, 0])
        hit &= left[:, :, None, None, 1] == right[:, None, :, None, 0]
        hit &= right[:, None, :, None, 1] == target[None, None, None, :, 1]
        return hit, left, target

    def order(need):
        flat = need.reshape(-1).astype(jnp.int32)
        return (jnp.cumsum(flat) - flat).reshape(need.shape)

    def picks(need, code, count):
        rank = order(need)
        slot = jnp.arange(count, dtype=jnp.int32)
        chosen = need[None] & (rank[None] == slot[:, None, None])
        return jnp.sum(jnp.where(chosen, code[None], 0), (1, 2))

    hit, left, target = links(this_row, this_col)
    near_right = (k % 2 == this_row % 2)[:, None]
    near_left = (k // 8 == this_col // 8)[:, None]
    slot = jnp.arange(SLOTS, dtype=jnp.int32)[None]
    right_place = (k // 2)[:, None] * SLOTS + slot
    left_place = (k % 8)[:, None] * SLOTS + slot

    other_right = jnp.any(links(this_row + 1 - 2 * (this_row % 2), this_col)[0], (1, 3))
    other_left = jnp.any(links(this_row, (this_col + 8) % n)[0], (2, 3))
    pack_right = picks(other_right & near_right, right_place, PACK)
    pack_left = picks(other_left & near_left, left_place, PACK)

    far_right = jnp.any(hit, (1, 3)) & ~near_right
    far_left = jnp.any(hit, (2, 3)) & ~near_left
    at_right = jnp.where(near_right, right_place, HALF + order(far_right))
    at_left = jnp.where(near_left, left_place, HALF + order(far_left))

    rank = order(hit)
    turn = jnp.arange(TRIPLES, dtype=jnp.int32)
    chosen = hit[None] & (rank[None] == turn[:, None, None, None, None])

    def of_turn(code):
        return jnp.sum(jnp.where(chosen, code[None], 0), (1, 2, 3, 4))

    s_index = jnp.arange(SLOTS, dtype=jnp.int32)
    target_at = of_turn(s_index[None, None, None, :])
    left_at = of_turn(at_left[:, :, None, None])
    right_at = of_turn(at_right[:, None, :, None])
    middle = of_turn((k[:, None] * tile + left[:, :, 1])[:, :, None, None])
    weight = jnp.any(chosen, (1, 2, 3)).astype(jnp.float32)
    whole = jnp.concatenate([target_at, left_at, right_at, pack_right, pack_left])
    part = jnp.concatenate(
        [
            middle.astype(jnp.float32),
            (this_row * tile + target[:, 0]).astype(jnp.float32),
            (this_col * tile + target[:, 1]).astype(jnp.float32),
            weight.reshape(-1),
        ]
    )
    return whole, part


AT_LEFT = TRIPLES
AT_RIGHT = 2 * TRIPLES
AT_PACK_RIGHT = 3 * TRIPLES
AT_PACK_LEFT = 3 * TRIPLES + PACK
AT_ROW = TRIPLES
AT_COL = TRIPLES + SLOTS
AT_WEIGHT = TRIPLES + 2 * SLOTS
AT_SPREAD = AT_WEIGHT + TRIPLES * SLOTS
LINES = AT_SPREAD + 2


def remote(src, dst, sent, came, row, col):
    return pltpu.make_async_remote_copy(
        src_ref=src,
        dst_ref=dst,
        send_sem=sent,
        recv_sem=came,
        device_id=(row, col),
        device_id_type=MESH,
    )


def kernel(
    whole,
    part,
    core_ref,
    band_ref,
    out_ref,
    bands,
    right_pool,
    left_pool,
    square_pool,
    right_out,
    right_in,
    left_out,
    left_in,
    square_out,
    square_in,
    fock,
    square,
    row_vec,
    col_vec,
    mid_vec,
    left_used,
    right_used,
    z_sent,
    z_came,
    x_sent,
    x_came,
    c_sent,
    c_came,
    y_sent,
    y_came,
    b_sent,
    b_came,
):
    row = lax.axis_index("row")
    col = lax.axis_index("col")
    z, y_lo = row // 2, row % 2
    x, core = col // 2 % NX, col % 2
    z_rows = ((row + 2) % 16, (row + 14) % 16)
    y_row = row + 1 - 2 * y_lo
    base = col - x * 2
    x_cols = (base + (x + 1) % NX * 2, base + (x + NX - 1) % NX * 2)
    core_col = col + 1 - 2 * core
    far_col = (col + 8) % 16

    gate = pltpu.get_barrier_semaphore()
    greet = [(z_rows[0], col), (z_rows[1], col), (y_row, col)]
    greet += [(row, (col + step) % 16) for step in range(1, 16)]
    for partner in greet:
        pl.semaphore_signal(gate, inc=1, device_id=partner, device_id_type=MESH)
    pl.semaphore_wait(gate, len(greet))

    started = []

    def send(copy):
        copy.start()
        started.append(copy)

    def z_tile(way, distance):
        return (z + (NZ - distance if way == 0 else distance)) % NZ

    def z_copy(way, d, b, incoming):
        tile = z_tile(way, d if incoming else d - 1)
        place = right_pool.at[tile * SLOTS + b]
        src = core_ref.at[b] if d == 1 and not incoming else place
        sems = z_sent.at[way, d - 1, b], z_came.at[way, d - 1, b]
        return remote(src, place, *sems, z_rows[way], col)

    def z_has(way, d, b):
        return d < 4 or (d == 4 and b // 2 == way)

    def z_take(d, b):
        for way in range(2):
            if z_has(way, d, b):
                z_copy(way, d, b, True).wait_recv()
                if z_has(way, d + 1, b):
                    send(z_copy(way, d + 1, b, False))

    def x_tile(way, distance):
        return (x + (NX - distance if way == 0 else distance)) % NX * 2 + core

    def x_copy(own, pool, turn, way, d, b, incoming):
        tile = x_tile(way, d if incoming else d - 1)
        place = pool.at[tile * SLOTS + b]
        src = own.at[b] if d == 1 and not incoming else place
        sems = x_sent.at[turn, way, d - 1, b], x_came.at[turn, way, d - 1, b]
        return remote(src, place, *sems, row, x_cols[way])

    def x_has(way, d, b):
        return d < 2 or (d == 2 and b // 2 == way)

    def x_take(own, pool, turn, d, b):
        for way in range(2):
            if x_has(way, d, b):
                x_copy(own, pool, turn, way, d, b, True).wait_recv()
                if x_has(way, d + 1, b):
                    send(x_copy(own, pool, turn, way, d + 1, b, False))

    def c_copy(own, pool, turn, at, incoming):
        tile = (x + at) % NX * 2
        tile = tile + (1 - core if incoming else core)
        place = pool.at[pl.ds(tile * SLOTS, SLOTS)]
        src = own if at == 0 and not incoming else place
        return remote(src, place, c_sent.at[turn, at], c_came.at[turn, at], row, core_col)

    def x_start(own, pool, turn):
        for b in range(SLOTS):
            for way in range(2):
                send(x_copy(own, pool, turn, way, 1, b, False))
        send(c_copy(own, pool, turn, 0, False))

    def pack(pool, staging, first):
        for j in range(PACK):
            staging[j] = pool[whole[first + j]]

    def y_copy(staging, landing, turn, there):
        return remote(staging, landing, y_sent.at[turn], y_came.at[turn], *there)

    def band_copy(step, incoming):
        owner = (col + 16 - step) % 16 if incoming else col
        place = bands.at[owner]
        src = place if incoming else band_ref
        sems = b_sent.at[step - 1], b_came.at[step - 1]
        return remote(src, place, *sems, row, (col + step) % 16)

    for b in range(SLOTS):
        for way in range(2):
            send(z_copy(way, 1, b, False))
    for step in range(1, 16):
        send(band_copy(step, False))
    x_start(core_ref, left_pool, 0)

    bands[col] = band_ref[...]
    right_pool[pl.ds(z * SLOTS, SLOTS)] = core_ref[...]
    left_pool[pl.ds((x * 2 + core) * SLOTS, SLOTS)] = core_ref[...]

    for b in range(SLOTS):
        z_take(1, b)
        x_take(core_ref, left_pool, 0, 1, b)
    send(c_copy(core_ref, left_pool, 0, 1, False))
    send(c_copy(core_ref, left_pool, 0, 3, False))

    for step in range(1, 16):
        band_copy(step, True).wait_recv()

    def vectors_on(block):
        return jnp.sum(jnp.where(bands[:, 1] == block, bands[:, 0], 0.0), axis=1)

    def outer(left, right):
        return lax.dot_general(
            left,
            right,
            (((0,), (0,)), ((), ())),
            precision=highest,
            preferred_element_type=jnp.float32,
        )

    for s in range(SLOTS):
        row_vec[s] = vectors_on(part[AT_ROW + s])
        col_vec[s] = vectors_on(part[AT_COL + s])

    z_take(2, 0)
    z_take(2, 1)
    for t in range(TRIPLES):
        mid_vec[t] = vectors_on(part[t])
    z_take(2, 2)
    z_take(2, 3)

    for b in range(SLOTS):
        x_take(core_ref, left_pool, 0, 2, b)
    send(c_copy(core_ref, left_pool, 0, 2, False))
    for at in range(NX):
        c_copy(core_ref, left_pool, 0, at, True).wait_recv()
    pack(left_pool, left_out, AT_PACK_LEFT)
    send(y_copy(left_out, left_in, 0, (row, far_col)))

    for s in range(SLOTS):
        fock[s] = core_ref[s] - outer(row_vec[s], col_vec[s])

    for b in range(SLOTS):
        z_take(3, b)

    def pooled(pool, landing, at):
        near = pool[jnp.minimum(at, HALF - 1)]
        far = landing[jnp.maximum(at - HALF, 0)]
        return jnp.where(at < HALF, near, far)

    inverse = part[AT_SPREAD + 1]
    y_copy(left_out, left_in, 0, (row, far_col)).wait_recv()
    for t in range(TRIPLES):
        block = pooled(left_pool, left_in, whole[AT_LEFT + t])
        left_used[t] = (block - outer(row_vec[whole[t]], mid_vec[t])) * inverse

    for b in range(SLOTS):
        z_take(4, b)
    pack(right_pool, right_out, AT_PACK_RIGHT)
    send(y_copy(right_out, right_in, 1, (y_row, col)))
    y_copy(right_out, right_in, 1, (y_row, col)).wait_recv()

    def product(left, right):
        return jnp.dot(left, right, precision=highest, preferred_element_type=jnp.float32)

    def weighted(target, blocks):
        total = blocks[0] * part[AT_WEIGHT + target]
        for t in range(1, TRIPLES):
            total = total + blocks[t] * part[AT_WEIGHT + t * SLOTS + target]
        return total

    for t in range(TRIPLES):
        block = pooled(right_pool, right_in, whole[AT_RIGHT + t])
        right_used[t] = (block - outer(mid_vec[t], col_vec[whole[t]])) * inverse
        left_used[t] = product(left_used[t], right_used[t])
    for s in range(SLOTS):
        square[s] = weighted(s, left_used)

    x_start(square, square_pool, 1)
    square_pool[pl.ds((x * 2 + core) * SLOTS, SLOTS)] = square[...]
    for b in range(SLOTS):
        x_take(square, square_pool, 1, 1, b)
    send(c_copy(square, square_pool, 1, 1, False))
    send(c_copy(square, square_pool, 1, 3, False))
    for b in range(SLOTS):
        x_take(square, square_pool, 1, 2, b)
    send(c_copy(square, square_pool, 1, 2, False))
    for at in range(NX):
        c_copy(square, square_pool, 1, at, True).wait_recv()
    pack(square_pool, square_out, AT_PACK_LEFT)
    send(y_copy(square_out, square_in, 2, (row, far_col)))
    y_copy(square_out, square_in, 2, (row, far_col)).wait_recv()

    for t in range(TRIPLES):
        block = pooled(square_pool, square_in, whole[AT_LEFT + t])
        left_used[t] = product(block, right_used[t])
    for s in range(SLOTS):
        cube = weighted(s, left_used)
        out_ref[s] = 1.5 * fock[s] - (2.0 * part[AT_SPREAD]) * cube

    for copy in started:
        copy.wait_send()


def sparse(core_blocks, whole, part, band_vectors, band_blocks):
    blocks = band_blocks.astype(jnp.float32)[:, :, None]
    message = jnp.stack([band_vectors[0], jnp.broadcast_to(blocks[0], band_vectors.shape[1:])])
    support = band_vectors.shape[1]
    f32 = jnp.float32
    block = (BS, BS)
    smem = pl.BlockSpec(memory_space=pltpu.SMEM)
    vmem = pl.BlockSpec(memory_space=pltpu.VMEM)
    dma = pltpu.SemaphoreType.DMA
    return pl.pallas_call(
        kernel,
        out_shape=jax.ShapeDtypeStruct(core_blocks.shape, f32),
        in_specs=[smem, smem, vmem, vmem],
        out_specs=vmem,
        scratch_shapes=[
            pltpu.VMEM((16, 2, support, BS), f32),
            pltpu.VMEM((HALF, *block), f32),
            pltpu.VMEM((HALF, *block), f32),
            pltpu.VMEM((HALF, *block), f32),
            pltpu.VMEM((PACK, *block), f32),
            pltpu.VMEM((PACK, *block), f32),
            pltpu.VMEM((PACK, *block), f32),
            pltpu.VMEM((PACK, *block), f32),
            pltpu.VMEM((PACK, *block), f32),
            pltpu.VMEM((PACK, *block), f32),
            pltpu.VMEM((SLOTS, *block), f32),
            pltpu.VMEM((SLOTS, *block), f32),
            pltpu.VMEM((SLOTS, 16, BS), f32),
            pltpu.VMEM((SLOTS, 16, BS), f32),
            pltpu.VMEM((TRIPLES, 16, BS), f32),
            pltpu.VMEM((TRIPLES, *block), f32),
            pltpu.VMEM((TRIPLES, *block), f32),
            dma((2, 4, SLOTS)),
            dma((2, 4, SLOTS)),
            dma((2, 2, 2, SLOTS)),
            dma((2, 2, 2, SLOTS)),
            dma((2, NX)),
            dma((2, NX)),
            dma((3,)),
            dma((3,)),
            dma((15,)),
            dma((15,)),
        ],
        compiler_params=pltpu.CompilerParams(collective_id=0, has_side_effects=True),
        name="sparse",
    )(whole, part, core_blocks, message)


def on_device(core_blocks, block_coords, band_vectors, band_blocks, spread):
    row_count = lax.axis_size("row")
    column_count = lax.axis_size("col")
    layout = block_coords.reshape(row_count, SLOTS, column_count, 2)
    whole, part = plan_of(layout, lax.axis_index("row"), lax.axis_index("col"))
    part = jnp.concatenate([part, jnp.stack([spread, 1.0 / spread])])
    return lax.cond(
        fits(layout),
        lambda: sparse(core_blocks, whole, part, band_vectors, band_blocks),
        lambda: general(core_blocks, block_coords, band_vectors, band_blocks, spread),
    )


def solution(mesh):
    placed = (P("row", "col", None), P(), P("col", None, None), P("col", None), P())
    return jax.shard_map(
        on_device, mesh=mesh, in_specs=placed, out_specs=P("row", "col", None), check_vma=False
    )
```

```python
import functools

import jax
import jax.numpy as jnp
from jax import lax
from jax.experimental import pallas as pl
from jax.experimental.pallas import tpu as pltpu
from jax.sharding import PartitionSpec as P

NB = 160
BS = 128
SLOTS = 4
MESH = pl.DeviceIdType.MESH

NZ = 8
NX = 4
TILE = 10
ROOM = 20
PAD = 256

highest = lax.Precision.HIGHEST


def shifted(block, axis, distance):
    devices = range(lax.axis_size(axis))
    route = [((i - distance) % len(devices), i) for i in devices]
    return lax.ppermute(block, axis, route)


def exchange_term(vectors, blocks, block_rows, block_cols):
    hit_row = (blocks[:, :, None] == block_rows[None, None, :]).astype(jnp.float32)
    hit_col = (blocks[:, :, None] == block_cols[None, None, :]).astype(jnp.float32)
    vec_row = jnp.einsum("bln,blx->bnx", hit_row, vectors, precision=highest)
    vec_col = jnp.einsum("bln,blx->bnx", hit_col, vectors, precision=highest)
    return -jnp.einsum("bnx,bny->nxy", vec_row, vec_col, precision=highest)


def tile_layout(layout, tile_row, tile_col):
    slots = layout.shape[1]
    start = (tile_row, jnp.int32(0), tile_col, jnp.int32(0))
    return lax.dynamic_slice(layout, start, (1, slots, 1, 2)).reshape(slots, 2)


def link_weights(targets, left_local, piece, right_local, tile_rows):
    row_target = targets[:, None, None, 0]
    col_target = targets[:, None, None, 1]
    row_left = left_local[None, :, None, 0]
    col_left = left_local[None, :, None, 1]
    row_right = right_local[None, None, :, 0]
    col_right = right_local[None, None, :, 1]
    keep = (row_left == row_target) & (col_left // tile_rows == piece)
    keep = keep & (col_left % tile_rows == row_right) & (col_right == col_target)
    return keep.astype(jnp.float32)


def accumulate(
    total, targets, left_blocks, left_local, piece, right_blocks, right_local, tile_rows
):
    weight = link_weights(targets, left_local, piece, right_local, tile_rows)
    pairs = jnp.einsum("axk,bky->axby", left_blocks, right_blocks, precision=highest)
    return total + jnp.einsum("tab,axby->txy", weight, pairs, precision=highest)


def align(block, axis, amount):
    for place in range((lax.axis_size(axis) - 1).bit_length()):
        moved = shifted(block, axis, -(1 << place))
        block = jnp.where(amount >> place & 1 == 1, moved, block)
    return block


def shifted_product(left, right, layout, targets, this_row, this_col, tile_rows):
    row_count = lax.axis_size("row")
    left = align(left, "col", this_row)

    def step_body(step, carry):
        total, left, right = carry
        source = (this_row + this_col + step) % row_count
        left_local = tile_layout(layout, this_row, source)
        right_local = tile_layout(layout, source, this_col)
        total = accumulate(
            total, targets, left, left_local, 0, right, right_local, tile_rows
        )
        left = shifted(left, "col", -1)
        right = shifted(right, "row", -1)
        return (total, left, right)

    total, left, right = lax.fori_loop(
        0, row_count, step_body, (jnp.zeros_like(left), left, right)
    )
    return (total, right)


def general(core_blocks, block_coords, band_vectors, band_blocks, spread):
    row_count = lax.axis_size("row")
    column_count = lax.axis_size("col")
    tile_rows = NB // row_count
    tile_columns = NB // column_count
    slots = core_blocks.shape[0]
    this_row = lax.axis_index("row")
    this_col = lax.axis_index("col")
    layout = block_coords.reshape(row_count, slots, column_count, 2)
    targets = tile_layout(layout, this_row, this_col)
    vectors, blocks = (
        lax.all_gather(band_vectors, "col", axis=0, tiled=True),
        lax.all_gather(band_blocks, "col", axis=0, tiled=True),
    )
    block_rows = this_row * tile_rows + targets[:, 0]
    block_cols = this_col * tile_columns + targets[:, 1]
    exchange = exchange_term(vectors, blocks, block_rows, block_cols)
    fock = core_blocks + exchange
    scaled = fock / spread
    right = align(scaled, "row", this_col)
    square, right = shifted_product(
        scaled, right, layout, targets, this_row, this_col, tile_rows
    )
    cube, right = shifted_product(
        square, right, layout, targets, this_row, this_col, tile_rows
    )
    return 1.5 * fock - 2.0 * spread * cube


def iota(shape, axis):
    return lax.broadcasted_iota(jnp.int32, shape, axis)


def ones_where(mask):
    return jnp.where(mask, 1.0, 0.0).astype(jnp.float32)


def times(left, right, precision=None):
    return jnp.dot(left, right, precision=precision, preferred_element_type=jnp.float32)


def outer(left, right):
    return lax.dot_general(
        left,
        right,
        (((0,), (0,)), ((), ())),
        precision=highest,
        preferred_element_type=jnp.float32,
    )


def most_products(coords):
    i, c = iota((PAD, 16), 0), iota((PAD, 16), 1)
    down = (i >= c * TILE) & (i < c * TILE + TILE)
    row_at = jnp.sum(jnp.where(down, i - c * TILE + 1, 0), axis=1, keepdims=True) - 1
    r, j = iota((16, PAD), 0), iota((16, PAD), 1)
    along = (j >= r * TILE) & (j < r * TILE + TILE)
    col_at = jnp.sum(jnp.where(along, j - r * TILE + 1, 0), axis=0, keepdims=True) - 1
    row_at, col_at = row_at.astype(jnp.float32), col_at.astype(jnp.float32)
    down, along = ones_where(down), ones_where(along)
    line, tile = iota((32, 16), 0), iota((32, 16), 1)
    rows = times(coords, ones_where(line == 2 * tile))
    cols = times(coords, ones_where(line == 2 * tile + 1))
    pattern = jnp.zeros((PAD, PAD), jnp.float32)
    for s in range(SLOTS):
        of_slot = ones_where(iota((16, 64), 1) == iota((16, 64), 0) * SLOTS + s)
        q = times(times(down, times(of_slot, rows)), along)
        p = times(times(down, times(of_slot, cols)), along)
        pattern = jnp.where((q == row_at) & (p == col_at), 1.0, pattern)
    links = pattern * times(pattern, pattern)
    return jnp.max(times(times(along, links), down))


def products_here(coords, row, col):
    line, lane = iota((64, 32), 0), iota((64, 32), 1)
    high, wide = iota((64, 64), 0), iota((64, 64), 1)
    i, pair = iota((64, 16), 0), iota((64, 16), 1)

    def at_lane(array, place):
        return jnp.sum(jnp.where(lane == place, array, 0.0), axis=1, keepdims=True)

    strip = times(ones_where(wide == row * SLOTS + (high & 3)), coords)
    left_row = at_lane(strip, (line >> 2) * 2)
    left_col = at_lane(strip, (line >> 2) * 2 + 1)
    here_row, here_col = at_lane(coords, col * 2), at_lane(coords, col * 2 + 1)
    same_tile = ones_where((high >> 2) == (wide >> 2))
    of_right = (i & 3) == (pair >> 2)
    right_row = times(same_tile, jnp.where(of_right, here_row, 0.0))
    right_col = times(same_tile, jnp.where(of_right, here_col, 0.0))
    of_target = i == row * SLOTS + (pair & 3)
    everywhere = jnp.ones((64, 64), jnp.float32)
    target_row = times(everywhere, jnp.where(of_target, here_row, 0.0))
    target_col = times(everywhere, jnp.where(of_target, here_col, 0.0))
    hit = (left_row == target_row) & (left_col == right_row) & (right_col == target_col)
    found = ones_where(hit)
    in_line = jnp.broadcast_to(jnp.sum(found, axis=1, keepdims=True), (64, 16))
    before = ones_where(iota((16, 16), 0) < iota((16, 16), 1))
    rank = times(ones_where(wide < high), in_line) + times(found, before)
    rank = jnp.where(hit, rank, -1.0)
    code = (i * 16 + pair).astype(jnp.float32) + 1024.0 * left_col
    number = jnp.sum(found)
    codes = [jnp.sum(jnp.where(rank == float(t), code, 0.0)) for t in range(ROOM)]
    return number, [c.astype(jnp.int32) for c in codes]


def kernel(
    spread,
    coords_ref,
    core_ref,
    vector_ref,
    block_ref,
    out_ref,
    most_ref,
    message,
    bands,
    right_pool,
    left_pool,
    square_pool,
    fock,
    square,
    row_vec,
    col_vec,
    mid_vec,
    left_used,
    right_used,
    sent,
    z_came,
    y_came,
    far_came,
    x_came,
    c_came,
    b_came,
    far2_came,
    x2_came,
    c2_came,
):
    row = lax.axis_index("row")
    col = lax.axis_index("col")
    z, y_lo = row // 2, row % 2
    y_hi, x, core = col // 8, col // 2 % NX, col % 2
    z_rows = ((row + 2) % 16, (row + 14) % 16)
    y_row = row + 1 - 2 * y_lo
    base = col - x * 2
    x_cols = (base + (x + 1) % NX * 2, base + (x + NX - 1) % NX * 2)
    core_col = col + 1 - 2 * core
    far_col = (col + 8) % 16

    gate = pltpu.get_barrier_semaphore()
    greet = [(z_rows[0], col), (z_rows[1], col), (y_row, col)]
    greet += [(row, (col + step) % 16) for step in range(1, 16)]
    for partner in greet:
        pl.semaphore_signal(gate, inc=1, device_id=partner, device_id_type=MESH)

    support = vector_ref.shape[1]
    on_diagonal = iota((support, support), 0) == iota((support, support), 1)
    block_of = jnp.sum(jnp.where(on_diagonal, block_ref[...], 0), axis=1, keepdims=True)
    message[0] = vector_ref[0]
    message[1] = jnp.broadcast_to(block_of.astype(jnp.float32), (support, BS))
    bands[col] = message[...]
    right_pool[pl.ds(row * SLOTS, SLOTS)] = core_ref[...]
    left_pool[pl.ds(col * SLOTS, SLOTS)] = core_ref[...]

    pl.semaphore_wait(gate, len(greet))

    blocks_sent = [0, 0, 0, 0]

    def remote(src, dst, came, to_row, to_col, kind):
        return pltpu.make_async_remote_copy(
            src_ref=src,
            dst_ref=dst,
            send_sem=sent.at[kind],
            recv_sem=came,
            device_id=(to_row, to_col),
            device_id_type=MESH,
        )

    def send(copy, blocks, kind):
        copy.start()
        blocks_sent[kind] += blocks

    OWN_LATE, OWN_EARLY, FAR_EARLY = (2, 0), (0, 0), (0, 1)
    ITEMS = (OWN_LATE, OWN_EARLY, FAR_EARLY)

    def turned(at, size, way, distance):
        return (at + (size - distance if way == 0 else distance)) % size

    def span(first, way, last):
        return (first + way, 1) if last else (first, 2)

    def z_copy(way, d, item, incoming):
        first, far = item
        tile = turned(z, NZ, way, d if incoming else d - 1)
        plane = 1 - y_lo if far else y_lo
        at, size = span(first, way, d == 4)
        place = right_pool.at[pl.ds((tile * 2 + plane) * SLOTS + at, size)]
        own = d == 1 and not far and not incoming
        src = core_ref.at[pl.ds(at, size)] if own else place
        came = z_came.at[way, d - 1, ITEMS.index(item)]
        return remote(src, place, came, z_rows[way], col, 0), size, 0

    def y_copy(way, d, first, incoming):
        tile = z if d == 0 else turned(z, NZ, way, d)
        plane = 1 - y_lo if incoming else y_lo
        at, size = span(first, way, d == 4)
        place = right_pool.at[pl.ds((tile * 2 + plane) * SLOTS + at, size)]
        src = core_ref.at[pl.ds(at, size)] if d == 0 and not incoming else place
        came = y_came.at[way, d] if d else y_came.at[first // 2, 0]
        return remote(src, place, came, y_row, col, 1), size, 1

    def z_take(d, item):
        for way in range(2):
            z_copy(way, d, item, True)[0].wait_recv()
            if d < 4:
                send(*z_copy(way, d + 1, item, False))
            if item == OWN_LATE:
                send(*y_copy(way, d, 2, False))

    def left_tile(way, d, far):
        return ((1 - y_hi if far else y_hi) * 8) + turned(x, NX, way, d) * 2

    def c_send(own, pool, came, way, d, far, at, size):
        kind = 2 if pool is left_pool else 3
        place = pool.at[pl.ds((left_tile(way, d, far) + core) * SLOTS + at, size)]
        src = own.at[pl.ds(at, size)] if d == 0 and not far else place
        send(remote(src, place, came.at[0], row, core_col, kind), size, kind)

    def c_wait(pool, came):
        place = pool.at[pl.ds(0, 32)]
        remote(place, place, came.at[0], row, core_col, 2).wait_recv()

    def far_whole(incoming):
        place = left_pool.at[pl.ds((left_tile(0, 0, incoming) + core) * SLOTS, SLOTS)]
        src = place if incoming else core_ref
        return remote(src, place, far_came.at[0], row, far_col, 1), SLOTS, 1

    def x_whole(way, d, far, incoming):
        tile = left_tile(way, d if incoming else d - 1, far) + core
        at, size = (0, SLOTS) if d == 1 else (2 * way, 2)
        place = left_pool.at[pl.ds(tile * SLOTS + at, size)]
        src = core_ref if d == 1 and not far and not incoming else place
        return remote(src, place, x_came.at[way, d - 1, far], row, x_cols[way], 1), size, 1

    def x_take(d, far):
        for way in range(2):
            x_whole(way, d, far, True)[0].wait_recv()
            if d == 1:
                send(*x_whole(way, 2, far, False))
            at, size = (0, SLOTS) if d == 1 else (2 * way, 2)
            c_send(core_ref, left_pool, c_came, way, d, far, at, size)

    send(*y_copy(0, 0, 0, False))
    for way in range(2):
        send(*z_copy(way, 1, OWN_LATE, False))
    send(*y_copy(0, 0, 2, False))
    for way in range(2):
        send(*z_copy(way, 1, OWN_EARLY, False))

    def band_copy(step):
        return pltpu.make_async_remote_copy(
            src_ref=message,
            dst_ref=bands.at[col],
            send_sem=sent.at[4],
            recv_sem=b_came.at[0],
            device_id=(row, (col + step) % 16),
            device_id_type=MESH,
        )

    for step in range(1, 16):
        band_copy(step).start()
    send(*far_whole(False))
    for way in range(2):
        send(*x_whole(way, 1, 0, False))
    c_send(core_ref, left_pool, c_came, 0, 0, 0, 0, SLOTS)

    coords = coords_ref[...].astype(jnp.float32)
    number, codes = products_here(coords, row, col)

    y_copy(0, 0, 0, True)[0].wait_recv()
    for way in range(2):
        send(*z_copy(way, 1, FAR_EARLY, False))

    most_ref[0] = most_products(coords)

    z_take(1, OWN_LATE)

    at_line, at_lane = iota((64, 32), 0), iota((64, 32), 1)

    def coordinate(s, which):
        mask = (at_line == row * SLOTS + s) & (at_lane == col * 2 + which)
        return jnp.sum(jnp.where(mask, coords, 0.0))

    def vectors_on(block):
        return jnp.sum(jnp.where(bands[:, 1] == block, bands[:, 0], 0.0), axis=1)

    many = bands.at[pl.ds(0, 15)]
    all_bands = pltpu.make_async_remote_copy(
        src_ref=many,
        dst_ref=many,
        send_sem=sent.at[4],
        recv_sem=b_came.at[0],
        device_id=(row, core_col),
        device_id_type=MESH,
    )
    all_bands.wait_recv()
    row_base, col_base = (row * TILE).astype(jnp.float32), (col * TILE).astype(jnp.float32)
    for s in range(SLOTS):
        row_vec[s] = vectors_on(row_base + coordinate(s, 0))
        col_vec[s] = vectors_on(col_base + coordinate(s, 1))

    left_at = [(c >> 4) & 63 for c in codes]
    right_at = [((c >> 6) & 15) * SLOTS + ((c >> 2) & 3) for c in codes]
    target_at = [c & 3 for c in codes]
    middle = [((c >> 6) & 15) * TILE + (c >> 10) for c in codes]

    def middles(first, last):
        for t in range(first, last):
            mid_vec[t] = vectors_on(middle[t].astype(jnp.float32))

    z_take(1, OWN_EARLY)
    x_take(1, 0)
    far_whole(True)[0].wait_recv()
    for way in range(2):
        send(*x_whole(way, 1, 1, False))
    c_send(core_ref, left_pool, c_came, 0, 0, 1, 0, SLOTS)
    middles(0, 5)
    z_take(1, FAR_EARLY)
    middles(5, 10)
    z_take(2, OWN_LATE)
    middles(10, 15)
    x_take(2, 0)
    x_take(1, 1)
    z_take(2, OWN_EARLY)
    middles(15, ROOM)
    z_take(2, FAR_EARLY)

    for s in range(SLOTS):
        fock[s] = core_ref[s] - outer(row_vec[s], col_vec[s])

    def right_terms(first, last):
        for t in range(first, last):
            right_used[t] = outer(mid_vec[t], col_vec[target_at[t]])

    right_terms(0, 10)
    z_take(3, OWN_LATE)
    right_terms(10, ROOM)
    x_take(2, 1)
    c_wait(left_pool, c_came)

    inverse = 1.0 / jnp.full((1, BS), spread[0], jnp.float32)
    scale = inverse * inverse

    def left_terms(first, last):
        for t in range(first, last):
            exchange = outer(row_vec[target_at[t]], mid_vec[t])
            left_used[t] = (left_pool[left_at[t]] - exchange) * scale

    left_terms(0, 6)
    z_take(3, OWN_EARLY)
    left_terms(6, 12)
    z_take(3, FAR_EARLY)
    left_terms(12, 16)
    z_take(4, OWN_LATE)
    left_terms(16, ROOM)
    z_take(4, OWN_EARLY)
    z_take(4, FAR_EARLY)
    y_copy(0, 0, 2, True)[0].wait_recv()
    for d in range(1, 5):
        for way in range(2):
            y_copy(way, d, 2, True)[0].wait_recv()

    def weight(t, s):
        live = (number > float(t)) & (target_at[t] == s)
        return jnp.where(live, 1.0, 0.0).astype(jnp.float32)

    weights = [[weight(t, s) for s in range(SLOTS)] for t in range(ROOM)]

    def weighted(s):
        total = left_used[0] * weights[0][s]
        for t in range(1, ROOM):
            total = total + left_used[t] * weights[t][s]
        return total

    for t in range(ROOM):
        block = right_pool[right_at[t]] - right_used[t]
        right_used[t] = block
        left_used[t] = times(left_used[t], block, highest)
    for s in range(SLOTS):
        square[s] = weighted(s)

    def far_copy(way, d, first, incoming):
        at, size = span(first, way, d == 2)
        tile = left_tile(way, d, incoming) + core
        place = square_pool.at[pl.ds(tile * SLOTS + at, size)]
        src = square.at[pl.ds(at, size)] if d == 0 and not incoming else place
        came = far2_came.at[way, d] if d else far2_came.at[first // 2, 0]
        return remote(src, place, came, row, far_col, 3), size, 3

    def x_copy(way, d, item, incoming):
        first, far = item
        at, size = span(first, way, d == 2)
        tile = left_tile(way, d if incoming else d - 1, far) + core
        place = square_pool.at[pl.ds(tile * SLOTS + at, size)]
        own = d == 1 and not far and not incoming
        src = square.at[pl.ds(at, size)] if own else place
        came = x2_came.at[way, d - 1, ITEMS.index(item)]
        return remote(src, place, came, row, x_cols[way], 3), size, 3

    def x2_take(d, item):
        first, far = item
        for way in range(2):
            x_copy(way, d, item, True)[0].wait_recv()
            if d == 1:
                send(*x_copy(way, 2, item, False))
            if item == OWN_LATE:
                send(*far_copy(way, d, 2, False))
            c_send(square, square_pool, c2_came, way, d, far, *span(first, way, d == 2))

    def far2_take(way, d, first):
        far_copy(way, d, first, True)[0].wait_recv()
        c_send(square, square_pool, c2_came, way, d, 1, *span(first, way, d == 2))

    send(*far_copy(0, 0, 0, False))
    for way in range(2):
        send(*x_copy(way, 1, OWN_LATE, False))
    send(*far_copy(0, 0, 2, False))
    for way in range(2):
        send(*x_copy(way, 1, OWN_EARLY, False))
    c_send(square, square_pool, c2_came, 0, 0, 0, 0, SLOTS)
    square_pool[pl.ds(col * SLOTS, SLOTS)] = square[...]
    x2_take(1, OWN_LATE)
    far2_take(0, 0, 0)
    for way in range(2):
        send(*x_copy(way, 1, FAR_EARLY, False))
    x2_take(1, OWN_EARLY)
    x2_take(2, OWN_LATE)
    far2_take(0, 0, 2)
    x2_take(1, FAR_EARLY)
    x2_take(2, OWN_EARLY)
    far2_take(0, 1, 2)
    far2_take(1, 1, 2)
    x2_take(2, FAR_EARLY)
    far2_take(0, 2, 2)
    far2_take(1, 2, 2)
    c_wait(square_pool, c2_came)

    for t in range(ROOM):
        left_used[t] = times(square_pool[left_at[t]], right_used[t], highest)
    for s in range(SLOTS):
        out_ref[s] = 1.5 * fock[s] - 2.0 * weighted(s)

    all_bands.wait_send()
    for kind, blocks in enumerate(blocks_sent):
        place = right_pool.at[pl.ds(0, blocks)]
        remote(place, place, far_came.at[0], row, core_col, kind).wait_send()


def sparse(core_blocks, block_coords, band_vectors, band_blocks, spread):
    support = band_vectors.shape[1]
    f32 = jnp.float32
    block = (BS, BS)
    smem = pl.BlockSpec(memory_space=pltpu.SMEM)
    vmem = pl.BlockSpec(memory_space=pltpu.VMEM)
    dma = pltpu.SemaphoreType.DMA
    return pl.pallas_call(
        kernel,
        out_shape=(
            jax.ShapeDtypeStruct(core_blocks.shape, f32),
            jax.ShapeDtypeStruct((1,), f32),
        ),
        in_specs=[smem, vmem, vmem, vmem, vmem],
        out_specs=(vmem, smem),
        scratch_shapes=[
            pltpu.VMEM((2, support, BS), f32),
            pltpu.VMEM((16, 2, support, BS), f32),
            pltpu.VMEM((64, *block), f32),
            pltpu.VMEM((64, *block), f32),
            pltpu.VMEM((64, *block), f32),
            pltpu.VMEM((SLOTS, *block), f32),
            pltpu.VMEM((SLOTS, *block), f32),
            pltpu.VMEM((SLOTS, 16, BS), f32),
            pltpu.VMEM((SLOTS, 16, BS), f32),
            pltpu.VMEM((ROOM, 16, BS), f32),
            pltpu.VMEM((ROOM, *block), f32),
            pltpu.VMEM((ROOM, *block), f32),
            dma((5,)),
            dma((2, 4, 3)),
            dma((2, 5)),
            dma((1,)),
            dma((2, 2, 2)),
            dma((1,)),
            dma((1,)),
            dma((2, 3)),
            dma((2, 2, 3)),
            dma((1,)),
        ],
        compiler_params=pltpu.CompilerParams(collective_id=0, has_side_effects=True),
        name="sparse",
    )(spread.reshape(1), block_coords, core_blocks, band_vectors, band_blocks)


def on_device(core_blocks, block_coords, band_vectors, band_blocks, spread):
    arguments = (core_blocks, block_coords, band_vectors, band_blocks, spread)
    purified, most = sparse(*arguments)
    return lax.cond(most[0] <= ROOM, lambda: purified, lambda: general(*arguments))


def solution(mesh):
    placed = (P("row", "col", None), P(), P("col", None, None), P("col", None), P())
    return jax.shard_map(
        on_device, mesh=mesh, in_specs=placed, out_specs=P("row", "col", None), check_vma=False
    )
```

```python
import functools

import jax
import jax.numpy as jnp
from jax import lax
from jax.experimental import pallas as pl
from jax.experimental.pallas import tpu as pltpu
from jax.sharding import PartitionSpec as P

NB = 160
BS = 128
SLOTS = 4
MESH = pl.DeviceIdType.MESH

NZ = 8
NX = 4
TILE = 10
ROOM = 20
PAD = 256

highest = lax.Precision.HIGHEST


def shifted(block, axis, distance):
    devices = range(lax.axis_size(axis))
    route = [((i - distance) % len(devices), i) for i in devices]
    return lax.ppermute(block, axis, route)


def exchange_term(vectors, blocks, block_rows, block_cols):
    hit_row = (blocks[:, :, None] == block_rows[None, None, :]).astype(jnp.float32)
    hit_col = (blocks[:, :, None] == block_cols[None, None, :]).astype(jnp.float32)
    vec_row = jnp.einsum("bln,blx->bnx", hit_row, vectors, precision=highest)
    vec_col = jnp.einsum("bln,blx->bnx", hit_col, vectors, precision=highest)
    return -jnp.einsum("bnx,bny->nxy", vec_row, vec_col, precision=highest)


def tile_layout(layout, tile_row, tile_col):
    slots = layout.shape[1]
    start = (tile_row, jnp.int32(0), tile_col, jnp.int32(0))
    return lax.dynamic_slice(layout, start, (1, slots, 1, 2)).reshape(slots, 2)


def link_weights(targets, left_local, piece, right_local, tile_rows):
    row_target = targets[:, None, None, 0]
    col_target = targets[:, None, None, 1]
    row_left = left_local[None, :, None, 0]
    col_left = left_local[None, :, None, 1]
    row_right = right_local[None, None, :, 0]
    col_right = right_local[None, None, :, 1]
    keep = (row_left == row_target) & (col_left // tile_rows == piece)
    keep = keep & (col_left % tile_rows == row_right) & (col_right == col_target)
    return keep.astype(jnp.float32)


def accumulate(
    total, targets, left_blocks, left_local, piece, right_blocks, right_local, tile_rows
):
    weight = link_weights(targets, left_local, piece, right_local, tile_rows)
    pairs = jnp.einsum("axk,bky->axby", left_blocks, right_blocks, precision=highest)
    return total + jnp.einsum("tab,axby->txy", weight, pairs, precision=highest)


def align(block, axis, amount):
    for place in range((lax.axis_size(axis) - 1).bit_length()):
        moved = shifted(block, axis, -(1 << place))
        block = jnp.where(amount >> place & 1 == 1, moved, block)
    return block


def shifted_product(left, right, layout, targets, this_row, this_col, tile_rows):
    row_count = lax.axis_size("row")
    left = align(left, "col", this_row)

    def step_body(step, carry):
        total, left, right = carry
        source = (this_row + this_col + step) % row_count
        left_local = tile_layout(layout, this_row, source)
        right_local = tile_layout(layout, source, this_col)
        total = accumulate(
            total, targets, left, left_local, 0, right, right_local, tile_rows
        )
        left = shifted(left, "col", -1)
        right = shifted(right, "row", -1)
        return (total, left, right)

    total, left, right = lax.fori_loop(
        0, row_count, step_body, (jnp.zeros_like(left), left, right)
    )
    return (total, right)


def general(core_blocks, block_coords, band_vectors, band_blocks, spread):
    row_count = lax.axis_size("row")
    column_count = lax.axis_size("col")
    tile_rows = NB // row_count
    tile_columns = NB // column_count
    slots = core_blocks.shape[0]
    this_row = lax.axis_index("row")
    this_col = lax.axis_index("col")
    layout = block_coords.reshape(row_count, slots, column_count, 2)
    targets = tile_layout(layout, this_row, this_col)
    vectors, blocks = (
        lax.all_gather(band_vectors, "col", axis=0, tiled=True),
        lax.all_gather(band_blocks, "col", axis=0, tiled=True),
    )
    block_rows = this_row * tile_rows + targets[:, 0]
    block_cols = this_col * tile_columns + targets[:, 1]
    exchange = exchange_term(vectors, blocks, block_rows, block_cols)
    fock = core_blocks + exchange
    scaled = fock / spread
    right = align(scaled, "row", this_col)
    square, right = shifted_product(
        scaled, right, layout, targets, this_row, this_col, tile_rows
    )
    cube, right = shifted_product(
        square, right, layout, targets, this_row, this_col, tile_rows
    )
    return 1.5 * fock - 2.0 * spread * cube


def iota(shape, axis):
    return lax.broadcasted_iota(jnp.int32, shape, axis)


def ones_where(mask):
    return jnp.where(mask, 1.0, 0.0).astype(jnp.float32)


def times(left, right, precision=None):
    return jnp.dot(left, right, precision=precision, preferred_element_type=jnp.float32)


def halves(block):
    high = block.astype(jnp.bfloat16)
    return high, (block - high.astype(jnp.float32)).astype(jnp.bfloat16)


def product(left_high, left_low, right_high, right_low):
    total = times(left_high, right_low) + times(left_low, right_high)
    return total + times(left_high, right_high)


def outer(left, right):
    return lax.dot_general(
        left,
        right,
        (((0,), (0,)), ((), ())),
        precision=highest,
        preferred_element_type=jnp.float32,
    )


def most_products(coords):
    i, c = iota((PAD, 16), 0), iota((PAD, 16), 1)
    down = (i >= c * TILE) & (i < c * TILE + TILE)
    row_at = jnp.sum(jnp.where(down, i - c * TILE + 1, 0), axis=1, keepdims=True) - 1
    r, j = iota((16, PAD), 0), iota((16, PAD), 1)
    along = (j >= r * TILE) & (j < r * TILE + TILE)
    col_at = jnp.sum(jnp.where(along, j - r * TILE + 1, 0), axis=0, keepdims=True) - 1
    row_at, col_at = row_at.astype(jnp.float32), col_at.astype(jnp.float32)
    down, along = ones_where(down), ones_where(along)
    line, tile = iota((32, 16), 0), iota((32, 16), 1)
    rows = times(coords, ones_where(line == 2 * tile))
    cols = times(coords, ones_where(line == 2 * tile + 1))
    pattern = jnp.zeros((PAD, PAD), jnp.float32)
    for s in range(SLOTS):
        of_slot = ones_where(iota((16, 64), 1) == iota((16, 64), 0) * SLOTS + s)
        q = times(times(down, times(of_slot, rows)), along)
        p = times(times(down, times(of_slot, cols)), along)
        pattern = jnp.where((q == row_at) & (p == col_at), 1.0, pattern)
    links = pattern * times(pattern, pattern)
    return jnp.max(times(times(along, links), down))


def products_here(coords, row, col):
    line, lane = iota((64, 32), 0), iota((64, 32), 1)
    high, wide = iota((64, 64), 0), iota((64, 64), 1)
    i, pair = iota((64, 16), 0), iota((64, 16), 1)

    def at_lane(array, place):
        return jnp.sum(jnp.where(lane == place, array, 0.0), axis=1, keepdims=True)

    strip = times(ones_where(wide == row * SLOTS + (high & 3)), coords)
    left_row = at_lane(strip, (line >> 2) * 2)
    left_col = at_lane(strip, (line >> 2) * 2 + 1)
    here_row, here_col = at_lane(coords, col * 2), at_lane(coords, col * 2 + 1)
    same_tile = ones_where((high >> 2) == (wide >> 2))
    of_right = (i & 3) == (pair >> 2)
    right_row = times(same_tile, jnp.where(of_right, here_row, 0.0))
    right_col = times(same_tile, jnp.where(of_right, here_col, 0.0))
    of_target = i == row * SLOTS + (pair & 3)
    everywhere = jnp.ones((64, 64), jnp.float32)
    target_row = times(everywhere, jnp.where(of_target, here_row, 0.0))
    target_col = times(everywhere, jnp.where(of_target, here_col, 0.0))
    hit = (left_row == target_row) & (left_col == right_row) & (right_col == target_col)
    found = ones_where(hit)
    in_line = jnp.broadcast_to(jnp.sum(found, axis=1, keepdims=True), (64, 16))
    before = ones_where(iota((16, 16), 0) < iota((16, 16), 1))
    rank = times(ones_where(wide < high), in_line) + times(found, before)
    rank = jnp.where(hit, rank, -1.0)
    code = (i * 16 + pair).astype(jnp.float32) + 1024.0 * left_col
    number = jnp.sum(found)
    codes = [jnp.sum(jnp.where(rank == float(t), code, 0.0)) for t in range(ROOM)]
    return number, [c.astype(jnp.int32) for c in codes]


def kernel(
    spread,
    coords_ref,
    core_ref,
    vector_ref,
    block_ref,
    out_ref,
    most_ref,
    message,
    bands,
    right_pool,
    left_pool,
    square_pool,
    fock,
    square,
    row_vec,
    col_vec,
    mid_vec,
    left_used,
    right_used,
    left_high,
    left_low,
    right_high,
    right_low,
    sent,
    z_came,
    y_came,
    far_came,
    x_came,
    c_came,
    b_came,
    far2_came,
    x2_came,
    c2_came,
):
    row = lax.axis_index("row")
    col = lax.axis_index("col")
    z, y_lo = row // 2, row % 2
    y_hi, x, core = col // 8, col // 2 % NX, col % 2
    z_rows = ((row + 2) % 16, (row + 14) % 16)
    y_row = row + 1 - 2 * y_lo
    base = col - x * 2
    x_cols = (base + (x + 1) % NX * 2, base + (x + NX - 1) % NX * 2)
    core_col = col + 1 - 2 * core
    far_col = (col + 8) % 16
    plane = [(row, y_hi * 8 + (col + step) % 8) for step in range(1, 8)]

    gate = pltpu.get_barrier_semaphore()
    greet = [(z_rows[0], col), (z_rows[1], col), (y_row, col)]
    greet += [(row, far_col)] + plane
    for partner in greet:
        pl.semaphore_signal(gate, inc=1, device_id=partner, device_id_type=MESH)

    support = vector_ref.shape[1]
    on_diagonal = iota((support, support), 0) == iota((support, support), 1)
    block_of = jnp.sum(jnp.where(on_diagonal, block_ref[...], 0), axis=1, keepdims=True)
    message[0] = vector_ref[0]
    message[1] = jnp.broadcast_to(block_of.astype(jnp.float32), (support, BS))

    pl.semaphore_wait(gate, len(greet))

    blocks_sent = [0, 0, 0, 0]

    def remote(src, dst, came, to_row, to_col, kind):
        return pltpu.make_async_remote_copy(
            src_ref=src,
            dst_ref=dst,
            send_sem=sent.at[kind],
            recv_sem=came,
            device_id=(to_row, to_col),
            device_id_type=MESH,
        )

    def send(copy, blocks, kind):
        copy.start()
        blocks_sent[kind] += blocks

    OWN_LATE, OWN_EARLY, FAR_EARLY = (2, 0), (0, 0), (0, 1)
    ITEMS = (OWN_LATE, OWN_EARLY, FAR_EARLY)

    def turned(at, size, way, distance):
        return (at + (size - distance if way == 0 else distance)) % size

    def span(first, way, last):
        return (first + way, 1) if last else (first, 2)

    def z_copy(way, d, item, incoming):
        first, far = item
        tile = turned(z, NZ, way, d if incoming else d - 1)
        plane = 1 - y_lo if far else y_lo
        at, size = span(first, way, d == 4)
        place = right_pool.at[pl.ds((tile * 2 + plane) * SLOTS + at, size)]
        own = d == 1 and not far and not incoming
        src = core_ref.at[pl.ds(at, size)] if own else place
        came = z_came.at[way, d - 1, ITEMS.index(item)]
        return remote(src, place, came, z_rows[way], col, 0), size, 0

    def y_copy(way, d, first, incoming):
        tile = z if d == 0 else turned(z, NZ, way, d)
        plane = 1 - y_lo if incoming else y_lo
        at, size = span(first, way, d == 4)
        place = right_pool.at[pl.ds((tile * 2 + plane) * SLOTS + at, size)]
        src = core_ref.at[pl.ds(at, size)] if d == 0 and not incoming else place
        came = y_came.at[way, d] if d else y_came.at[first // 2, 0]
        return remote(src, place, came, y_row, col, 1), size, 1

    def z_take(d, item):
        for way in range(2):
            z_copy(way, d, item, True)[0].wait_recv()
            if d < 4:
                send(*z_copy(way, d + 1, item, False))
            if item == OWN_LATE:
                send(*y_copy(way, d, 2, False))

    def left_tile(way, d, far):
        return ((1 - y_hi if far else y_hi) * 8) + turned(x, NX, way, d) * 2

    def c_send(own, pool, came, way, d, far, at, size):
        kind = 2 if pool is left_pool else 3
        place = pool.at[pl.ds((left_tile(way, d, far) + core) * SLOTS + at, size)]
        src = own.at[pl.ds(at, size)] if d == 0 and not far else place
        send(remote(src, place, came.at[0], row, core_col, kind), size, kind)

    def c_wait(pool, came):
        place = pool.at[pl.ds(0, 32)]
        remote(place, place, came.at[0], row, core_col, 2).wait_recv()

    def far_whole(incoming):
        place = left_pool.at[pl.ds((left_tile(0, 0, incoming) + core) * SLOTS, SLOTS)]
        src = place if incoming else core_ref
        return remote(src, place, far_came.at[0], row, far_col, 1), SLOTS, 1

    def x_whole(way, d, far, incoming):
        tile = left_tile(way, d if incoming else d - 1, far) + core
        at, size = (0, SLOTS) if d == 1 else (2 * way, 2)
        place = left_pool.at[pl.ds(tile * SLOTS + at, size)]
        src = core_ref if d == 1 and not far and not incoming else place
        return remote(src, place, x_came.at[way, d - 1, far], row, x_cols[way], 1), size, 1

    def x_take(d, far):
        for way in range(2):
            x_whole(way, d, far, True)[0].wait_recv()
            if d == 1:
                send(*x_whole(way, 2, far, False))
            at, size = (0, SLOTS) if d == 1 else (2 * way, 2)
            c_send(core_ref, left_pool, c_came, way, d, far, at, size)

    def band_copy(owner, to, came):
        return pltpu.make_async_remote_copy(
            src_ref=message if came or owner is col else bands.at[owner],
            dst_ref=bands.at[owner],
            send_sem=sent.at[4],
            recv_sem=b_came.at[came],
            device_id=to,
            device_id_type=MESH,
        )

    band_copy(col, (row, far_col), 1).start()
    send(*y_copy(0, 0, 0, False))
    for way in range(2):
        send(*z_copy(way, 1, OWN_LATE, False))
    for way in range(2):
        send(*x_whole(way, 1, 0, False))
    for way in range(2):
        send(*z_copy(way, 1, OWN_EARLY, False))
    send(*far_whole(False))

    for partner in plane:
        band_copy(col, partner, 0).start()
    send(*y_copy(0, 0, 2, False))
    c_send(core_ref, left_pool, c_came, 0, 0, 0, 0, SLOTS)
    bands[col] = message[...]
    right_pool[pl.ds(row * SLOTS, SLOTS)] = core_ref[...]
    left_pool[pl.ds(col * SLOTS, SLOTS)] = core_ref[...]

    unit = ones_where(iota((64, 64), 0) == iota((64, 64), 1))
    coords = lax.dot_general(
        unit,
        coords_ref[...].astype(jnp.float32),
        (((1,), (1,)), ((), ())),
        preferred_element_type=jnp.float32,
    )
    number, codes = products_here(coords, row, col)

    y_copy(0, 0, 0, True)[0].wait_recv()
    for way in range(2):
        send(*z_copy(way, 1, FAR_EARLY, False))

    at_line, at_lane = iota((64, 32), 0), iota((64, 32), 1)

    def coordinate(s, which):
        mask = (at_line == row * SLOTS + s) & (at_lane == col * 2 + which)
        return jnp.sum(jnp.where(mask, coords, 0.0))

    def vectors_on(block):
        return jnp.sum(jnp.where(bands[:, 1] == block, bands[:, 0], 0.0), axis=1)

    def all_bands(count):
        many = bands.at[pl.ds(0, count)]
        return pltpu.make_async_remote_copy(
            src_ref=many,
            dst_ref=many,
            send_sem=sent.at[4],
            recv_sem=b_came.at[0],
            device_id=(row, core_col),
            device_id_type=MESH,
        )

    row_base, col_base = (row * TILE).astype(jnp.float32), (col * TILE).astype(jnp.float32)

    left_at = [(c >> 4) & 63 for c in codes]
    right_at = [((c >> 6) & 15) * SLOTS + ((c >> 2) & 3) for c in codes]
    target_at = [c & 3 for c in codes]
    middle = [((c >> 6) & 15) * TILE + (c >> 10) for c in codes]

    def middles(first, last):
        for t in range(min(first, ROOM), min(last, ROOM)):
            mid_vec[t] = vectors_on(middle[t].astype(jnp.float32))

    def right_terms(first, last):
        for t in range(min(first, ROOM), min(last, ROOM)):
            right_used[t] = outer(mid_vec[t], col_vec[target_at[t]])

    inverse = 1.0 / jnp.full((1, BS), spread[0], jnp.float32)
    scale = inverse * inverse

    def left_terms(first, last):
        for t in range(min(first, ROOM), min(last, ROOM)):
            exchange = outer(row_vec[target_at[t]], mid_vec[t])
            high, low = halves((left_pool[left_at[t]] - exchange) * scale)
            left_high[t], left_low[t] = high, low

    z_take(1, OWN_LATE)
    band_copy(far_col, (row, far_col), 1).wait_recv()
    for partner in plane:
        band_copy(far_col, partner, 0).start()
    z_take(1, OWN_EARLY)
    x_take(1, 0)
    z_take(1, FAR_EARLY)
    x_take(2, 0)
    z_take(2, OWN_LATE)
    all_bands(14).wait_recv()
    for s in range(SLOTS):
        row_vec[s] = vectors_on(row_base + coordinate(s, 0))
        col_vec[s] = vectors_on(col_base + coordinate(s, 1))
    far_whole(True)[0].wait_recv()
    for way in range(2):
        send(*x_whole(way, 1, 1, False))
    c_send(core_ref, left_pool, c_came, 0, 0, 1, 0, SLOTS)
    middles(0, 10)
    z_take(2, OWN_EARLY)
    middles(10, ROOM)
    for s in range(SLOTS):
        fock[s] = core_ref[s] - outer(row_vec[s], col_vec[s])
    z_take(2, FAR_EARLY)
    right_terms(0, 10)
    z_take(3, OWN_LATE)
    right_terms(10, ROOM)
    x_take(1, 1)
    z_take(3, OWN_EARLY)
    most_ref[0] = most_products(coords)
    def weight(t, s):
        live = (number > float(t)) & (target_at[t] == s)
        return jnp.where(live, 1.0, 0.0).astype(jnp.float32)

    weights = [[weight(t, s) for s in range(SLOTS)] for t in range(ROOM)]

    z_take(3, FAR_EARLY)
    x_take(2, 1)
    z_take(4, OWN_LATE)
    c_wait(left_pool, c_came)
    left_terms(0, 10)
    z_take(4, OWN_EARLY)
    left_terms(10, ROOM)
    z_take(4, FAR_EARLY)
    y_copy(0, 0, 2, True)[0].wait_recv()
    for d in range(1, 5):
        for way in range(2):
            y_copy(way, d, 2, True)[0].wait_recv()

    def weighted(s):
        total = left_used[0] * weights[0][s]
        for t in range(1, ROOM):
            total = total + left_used[t] * weights[t][s]
        return total

    for t in range(ROOM):
        high, low = halves(right_pool[right_at[t]] - right_used[t])
        right_high[t], right_low[t] = high, low
        left_used[t] = product(left_high[t], left_low[t], high, low)
    for s in range(SLOTS):
        square[s] = weighted(s)

    def far_copy(way, d, first, incoming):
        at, size = span(first, way, d == 2)
        tile = left_tile(way, d, incoming) + core
        place = square_pool.at[pl.ds(tile * SLOTS + at, size)]
        src = square.at[pl.ds(at, size)] if d == 0 and not incoming else place
        came = far2_came.at[way, d] if d else far2_came.at[first // 2, 0]
        return remote(src, place, came, row, far_col, 3), size, 3

    def x_copy(way, d, item, incoming):
        first, far = item
        at, size = span(first, way, d == 2)
        tile = left_tile(way, d if incoming else d - 1, far) + core
        place = square_pool.at[pl.ds(tile * SLOTS + at, size)]
        own = d == 1 and not far and not incoming
        src = square.at[pl.ds(at, size)] if own else place
        came = x2_came.at[way, d - 1, ITEMS.index(item)]
        return remote(src, place, came, row, x_cols[way], 3), size, 3

    def x2_take(d, item):
        first, far = item
        for way in range(2):
            x_copy(way, d, item, True)[0].wait_recv()
            if d == 1:
                send(*x_copy(way, 2, item, False))
            if item == OWN_LATE:
                send(*far_copy(way, d, 2, False))
            c_send(square, square_pool, c2_came, way, d, far, *span(first, way, d == 2))

    def far2_take(way, d, first):
        far_copy(way, d, first, True)[0].wait_recv()
        c_send(square, square_pool, c2_came, way, d, 1, *span(first, way, d == 2))

    send(*far_copy(0, 0, 0, False))
    for way in range(2):
        send(*x_copy(way, 1, OWN_LATE, False))
    send(*far_copy(0, 0, 2, False))
    for way in range(2):
        send(*x_copy(way, 1, OWN_EARLY, False))
    c_send(square, square_pool, c2_came, 0, 0, 0, 0, SLOTS)
    square_pool[pl.ds(col * SLOTS, SLOTS)] = square[...]
    x2_take(1, OWN_LATE)
    far2_take(0, 0, 0)
    for way in range(2):
        send(*x_copy(way, 1, FAR_EARLY, False))
    x2_take(1, OWN_EARLY)
    x2_take(2, OWN_LATE)
    far2_take(0, 0, 2)
    x2_take(1, FAR_EARLY)
    x2_take(2, OWN_EARLY)
    far2_take(0, 1, 2)
    far2_take(1, 1, 2)
    x2_take(2, FAR_EARLY)
    far2_take(0, 2, 2)
    far2_take(1, 2, 2)
    c_wait(square_pool, c2_came)

    for t in range(ROOM):
        high, low = halves(square_pool[left_at[t]])
        left_used[t] = product(high, low, right_high[t], right_low[t])
    for s in range(SLOTS):
        out_ref[s] = 1.5 * fock[s] - 2.0 * weighted(s)

    all_bands(15).wait_send()
    for kind, blocks in enumerate(blocks_sent):
        place = right_pool.at[pl.ds(0, blocks)]
        remote(place, place, far_came.at[0], row, core_col, kind).wait_send()


def sparse(core_blocks, block_coords, band_vectors, band_blocks, spread):
    support = band_vectors.shape[1]
    f32 = jnp.float32
    block = (BS, BS)
    smem = pl.BlockSpec(memory_space=pltpu.SMEM)
    vmem = pl.BlockSpec(memory_space=pltpu.VMEM)
    dma = pltpu.SemaphoreType.DMA
    return pl.pallas_call(
        kernel,
        out_shape=(
            jax.ShapeDtypeStruct(core_blocks.shape, f32),
            jax.ShapeDtypeStruct((1,), f32),
        ),
        in_specs=[smem, vmem, vmem, vmem, vmem],
        out_specs=(vmem, smem),
        scratch_shapes=[
            pltpu.VMEM((2, support, BS), f32),
            pltpu.VMEM((16, 2, support, BS), f32),
            pltpu.VMEM((64, *block), f32),
            pltpu.VMEM((64, *block), f32),
            pltpu.VMEM((64, *block), f32),
            pltpu.VMEM((SLOTS, *block), f32),
            pltpu.VMEM((SLOTS, *block), f32),
            pltpu.VMEM((SLOTS, 16, BS), f32),
            pltpu.VMEM((SLOTS, 16, BS), f32),
            pltpu.VMEM((ROOM, 16, BS), f32),
            pltpu.VMEM((ROOM, *block), f32),
            pltpu.VMEM((ROOM, *block), f32),
            pltpu.VMEM((ROOM, *block), jnp.bfloat16),
            pltpu.VMEM((ROOM, *block), jnp.bfloat16),
            pltpu.VMEM((ROOM, *block), jnp.bfloat16),
            pltpu.VMEM((ROOM, *block), jnp.bfloat16),
            dma((5,)),
            dma((2, 4, 3)),
            dma((2, 5)),
            dma((1,)),
            dma((2, 2, 2)),
            dma((1,)),
            dma((2,)),
            dma((2, 3)),
            dma((2, 2, 3)),
            dma((1,)),
        ],
        compiler_params=pltpu.CompilerParams(
            collective_id=0, has_side_effects=True, vmem_limit_bytes=28 << 20
        ),
        name="sparse",
    )(spread.reshape(1), block_coords.T, core_blocks, band_vectors, band_blocks)


def on_device(core_blocks, block_coords, band_vectors, band_blocks, spread):
    arguments = (core_blocks, block_coords, band_vectors, band_blocks, spread)
    purified, most = sparse(*arguments)
    return lax.cond(most[0] <= ROOM, lambda: purified, lambda: general(*arguments))


def solution(mesh):
    placed = (P("row", "col", None), P(), P("col", None, None), P("col", None), P())
    return jax.shard_map(
        on_device, mesh=mesh, in_specs=placed, out_specs=P("row", "col", None), check_vma=False
    )
```

```python
import functools

import jax
import jax.numpy as jnp
from jax import lax
from jax.experimental import pallas as pl
from jax.experimental.pallas import tpu as pltpu
from jax.sharding import PartitionSpec as P

NB = 160
BS = 128
SLOTS = 4
MESH = pl.DeviceIdType.MESH

NZ = 8
NX = 4
TILE = 10
ROOM = 20
PAD = 256
ROWS = SLOTS * BS
EARLY = 240
EARLY_SQUARE = 272

highest = lax.Precision.HIGHEST


def shifted(block, axis, distance):
    devices = range(lax.axis_size(axis))
    route = [((i - distance) % len(devices), i) for i in devices]
    return lax.ppermute(block, axis, route)


def exchange_term(vectors, blocks, block_rows, block_cols):
    hit_row = (blocks[:, :, None] == block_rows[None, None, :]).astype(jnp.float32)
    hit_col = (blocks[:, :, None] == block_cols[None, None, :]).astype(jnp.float32)
    vec_row = jnp.einsum("bln,blx->bnx", hit_row, vectors, precision=highest)
    vec_col = jnp.einsum("bln,blx->bnx", hit_col, vectors, precision=highest)
    return -jnp.einsum("bnx,bny->nxy", vec_row, vec_col, precision=highest)


def tile_layout(layout, tile_row, tile_col):
    slots = layout.shape[1]
    start = (tile_row, jnp.int32(0), tile_col, jnp.int32(0))
    return lax.dynamic_slice(layout, start, (1, slots, 1, 2)).reshape(slots, 2)


def link_weights(targets, left_local, piece, right_local, tile_rows):
    row_target = targets[:, None, None, 0]
    col_target = targets[:, None, None, 1]
    row_left = left_local[None, :, None, 0]
    col_left = left_local[None, :, None, 1]
    row_right = right_local[None, None, :, 0]
    col_right = right_local[None, None, :, 1]
    keep = (row_left == row_target) & (col_left // tile_rows == piece)
    keep = keep & (col_left % tile_rows == row_right) & (col_right == col_target)
    return keep.astype(jnp.float32)


def accumulate(
    total, targets, left_blocks, left_local, piece, right_blocks, right_local, tile_rows
):
    weight = link_weights(targets, left_local, piece, right_local, tile_rows)
    pairs = jnp.einsum("axk,bky->axby", left_blocks, right_blocks, precision=highest)
    return total + jnp.einsum("tab,axby->txy", weight, pairs, precision=highest)


def align(block, axis, amount):
    for place in range((lax.axis_size(axis) - 1).bit_length()):
        moved = shifted(block, axis, -(1 << place))
        block = jnp.where(amount >> place & 1 == 1, moved, block)
    return block


def shifted_product(left, right, layout, targets, this_row, this_col, tile_rows):
    row_count = lax.axis_size("row")
    left = align(left, "col", this_row)

    def step_body(step, carry):
        total, left, right = carry
        source = (this_row + this_col + step) % row_count
        left_local = tile_layout(layout, this_row, source)
        right_local = tile_layout(layout, source, this_col)
        total = accumulate(
            total, targets, left, left_local, 0, right, right_local, tile_rows
        )
        left = shifted(left, "col", -1)
        right = shifted(right, "row", -1)
        return (total, left, right)

    total, left, right = lax.fori_loop(
        0, row_count, step_body, (jnp.zeros_like(left), left, right)
    )
    return (total, right)


def general(core_blocks, block_coords, band_vectors, band_blocks, spread):
    row_count = lax.axis_size("row")
    column_count = lax.axis_size("col")
    tile_rows = NB // row_count
    tile_columns = NB // column_count
    slots = core_blocks.shape[0]
    this_row = lax.axis_index("row")
    this_col = lax.axis_index("col")
    layout = block_coords.reshape(row_count, slots, column_count, 2)
    targets = tile_layout(layout, this_row, this_col)
    vectors, blocks = (
        lax.all_gather(band_vectors, "col", axis=0, tiled=True),
        lax.all_gather(band_blocks, "col", axis=0, tiled=True),
    )
    block_rows = this_row * tile_rows + targets[:, 0]
    block_cols = this_col * tile_columns + targets[:, 1]
    exchange = exchange_term(vectors, blocks, block_rows, block_cols)
    fock = core_blocks + exchange
    scaled = fock / spread
    right = align(scaled, "row", this_col)
    square, right = shifted_product(
        scaled, right, layout, targets, this_row, this_col, tile_rows
    )
    cube, right = shifted_product(
        square, right, layout, targets, this_row, this_col, tile_rows
    )
    return 1.5 * fock - 2.0 * spread * cube


def iota(shape, axis):
    return lax.broadcasted_iota(jnp.int32, shape, axis)


def ones_where(mask):
    return jnp.where(mask, 1.0, 0.0).astype(jnp.float32)


def times(left, right, precision=None):
    return jnp.dot(left, right, precision=precision, preferred_element_type=jnp.float32)


def halves(block):
    high = block.astype(jnp.bfloat16)
    return high, (block - high.astype(jnp.float32)).astype(jnp.bfloat16)


def product(left_high, left_low, right_high, right_low):
    total = times(left_high, right_low) + times(left_low, right_high)
    return total + times(left_high, right_high)


def outer(left, right):
    return lax.dot_general(
        left,
        right,
        (((0,), (0,)), ((), ())),
        precision=highest,
        preferred_element_type=jnp.float32,
    )


def most_products(coords):
    i, c = iota((PAD, 16), 0), iota((PAD, 16), 1)
    down = (i >= c * TILE) & (i < c * TILE + TILE)
    row_at = jnp.sum(jnp.where(down, i - c * TILE + 1, 0), axis=1, keepdims=True) - 1
    r, j = iota((16, PAD), 0), iota((16, PAD), 1)
    along = (j >= r * TILE) & (j < r * TILE + TILE)
    col_at = jnp.sum(jnp.where(along, j - r * TILE + 1, 0), axis=0, keepdims=True) - 1
    row_at, col_at = row_at.astype(jnp.float32), col_at.astype(jnp.float32)
    down, along = ones_where(down), ones_where(along)
    line, tile = iota((32, 16), 0), iota((32, 16), 1)
    rows = times(coords, ones_where(line == 2 * tile))
    cols = times(coords, ones_where(line == 2 * tile + 1))
    pattern = jnp.zeros((PAD, PAD), jnp.float32)
    for s in range(SLOTS):
        of_slot = ones_where(iota((16, 64), 1) == iota((16, 64), 0) * SLOTS + s)
        q = times(times(down, times(of_slot, rows)), along)
        p = times(times(down, times(of_slot, cols)), along)
        pattern = jnp.where((q == row_at) & (p == col_at), 1.0, pattern)
    links = pattern * times(pattern, pattern)
    return jnp.max(times(times(along, links), down))


def products_here(coords, row, col):
    line, lane = iota((64, 32), 0), iota((64, 32), 1)
    high, wide = iota((64, 64), 0), iota((64, 64), 1)
    i, pair = iota((64, 16), 0), iota((64, 16), 1)

    def at_lane(array, place):
        return jnp.sum(jnp.where(lane == place, array, 0.0), axis=1, keepdims=True)

    strip = times(ones_where(wide == row * SLOTS + (high & 3)), coords)
    left_row = at_lane(strip, (line >> 2) * 2)
    left_col = at_lane(strip, (line >> 2) * 2 + 1)
    here_row, here_col = at_lane(coords, col * 2), at_lane(coords, col * 2 + 1)
    same_tile = ones_where((high >> 2) == (wide >> 2))
    of_right = (i & 3) == (pair >> 2)
    right_row = times(same_tile, jnp.where(of_right, here_row, 0.0))
    right_col = times(same_tile, jnp.where(of_right, here_col, 0.0))
    of_target = i == row * SLOTS + (pair & 3)
    everywhere = jnp.ones((64, 64), jnp.float32)
    target_row = times(everywhere, jnp.where(of_target, here_row, 0.0))
    target_col = times(everywhere, jnp.where(of_target, here_col, 0.0))
    hit = (left_row == target_row) & (left_col == right_row) & (right_col == target_col)
    found = ones_where(hit)
    in_line = jnp.broadcast_to(jnp.sum(found, axis=1, keepdims=True), (64, 16))
    before = ones_where(iota((16, 16), 0) < iota((16, 16), 1))
    rank = times(ones_where(wide < high), in_line) + times(found, before)
    rank = jnp.where(hit, rank, -1.0)
    code = (i * 16 + pair).astype(jnp.float32) + 1024.0 * left_col
    number = jnp.sum(found)
    codes = [jnp.sum(jnp.where(rank == float(t), code, 0.0)) for t in range(ROOM)]
    return number, [c.astype(jnp.int32) for c in codes]


def kernel(
    spread_hbm,
    coords_hbm,
    core_hbm,
    vector_hbm,
    block_hbm,
    out_ref,
    fits_ref,
    kept_ref,
    spread,
    coords_ref,
    vector_ref,
    block_ref,
    came,
    fits_here,
    message,
    bands,
    right_pool,
    left_pool,
    square_pool,
    fock,
    square,
    row_vec,
    col_vec,
    mid_vec,
    left_used,
    right_used,
    left_high,
    left_low,
    right_high,
    right_low,
    sent,
    z_came,
    y_came,
    far_came,
    x_came,
    c_came,
    b_came,
    far2_came,
    x2_came,
    c2_came,
):
    row = lax.axis_index("row")
    col = lax.axis_index("col")
    z, y_lo = row // 2, row % 2
    y_hi, x, core = col // 8, col // 2 % NX, col % 2
    z_rows = ((row + 2) % 16, (row + 14) % 16)
    y_row = row + 1 - 2 * y_lo
    base = col - x * 2
    x_cols = (base + (x + 1) % NX * 2, base + (x + NX - 1) % NX * 2)
    core_col = col + 1 - 2 * core
    far_col = (col + 8) % 16
    plane = [(row, y_hi * 8 + (col + step) % 8) for step in range(1, 8)]

    gate = pltpu.get_barrier_semaphore()
    greet = [(z_rows[0], col), (z_rows[1], col), (y_row, col)]
    greet += [(row, far_col)] + plane
    for partner in greet:
        pl.semaphore_signal(gate, inc=1, device_id=partner, device_id_type=MESH)

    tile_rows = pl.ds(pl.multiple_of(row * ROWS, ROWS), ROWS)
    tile_cols = pl.ds(pl.multiple_of(col * ROWS, ROWS), ROWS)
    local = [
        pltpu.make_async_copy(vector_hbm, vector_ref, came.at[0]),
        pltpu.make_async_copy(block_hbm, block_ref, came.at[1]),
        pltpu.make_async_copy(coords_hbm, coords_ref, came.at[2]),
        pltpu.make_async_copy(spread_hbm, spread, came.at[3]),
        pltpu.make_async_copy(core_hbm, right_pool.at[tile_rows], came.at[4]),
        pltpu.make_async_copy(core_hbm, left_pool.at[tile_cols], came.at[5]),
        pltpu.make_async_copy(core_hbm, fock, came.at[6]),
    ]
    for copy in local:
        copy.start()
    pl.semaphore_wait(gate, len(greet))

    rows_sent = [0, 0, 0, 0]

    def remote(src, dst, came, to_row, to_col, kind):
        return pltpu.make_async_remote_copy(
            src_ref=src,
            dst_ref=dst,
            send_sem=sent.at[kind],
            recv_sem=came,
            device_id=(to_row, to_col),
            device_id_type=MESH,
        )

    def send(copy, rows, kind):
        copy.start()
        rows_sent[kind] += rows

    OWN_LATE, OWN_EARLY, FAR_EARLY = (1, 0), (0, 0), (0, 1)
    ITEMS = (OWN_LATE, OWN_EARLY, FAR_EARLY)

    def turned(at, size, way, distance):
        return (at + (size - distance if way == 0 else distance)) % size

    def span(late, early, way, last):
        at, size = (early, ROWS - early) if late else (0, early)
        return (at + way * (size // 2), size // 2) if last else (at, size)

    def rows_of(pool, tile, at, size):
        return pool.at[pl.ds(pl.multiple_of(tile * ROWS + at, 8), size)]

    def z_copy(way, d, item, incoming):
        late, far = item
        tile = turned(z, NZ, way, d if incoming else d - 1)
        plane = 1 - y_lo if far else y_lo
        at, size = span(late, EARLY, way, d == 4)
        place = rows_of(right_pool, tile * 2 + plane, at, size)
        own = d == 1 and not far and not incoming
        src = core_hbm.at[pl.ds(at, size)] if own else place
        came = z_came.at[way, d - 1, ITEMS.index(item)]
        return remote(src, place, came, z_rows[way], col, 0), size, 0

    def y_copy(way, d, late, incoming):
        tile = z if d == 0 else turned(z, NZ, way, d)
        plane = 1 - y_lo if incoming else y_lo
        at, size = span(late, EARLY, way, d == 4)
        place = rows_of(right_pool, tile * 2 + plane, at, size)
        src = core_hbm.at[pl.ds(at, size)] if d == 0 and not incoming else place
        came = y_came.at[way, d] if d else y_came.at[late, 0]
        return remote(src, place, came, y_row, col, 1), size, 1

    def z_take(d, item):
        for way in range(2):
            z_copy(way, d, item, True)[0].wait_recv()
            if d < 4:
                send(*z_copy(way, d + 1, item, False))
            if item == OWN_LATE:
                send(*y_copy(way, d, 1, False))

    def left_tile(way, d, far):
        return ((1 - y_hi if far else y_hi) * 8) + turned(x, NX, way, d) * 2

    def c_send(own, pool, came, way, d, far, at, size):
        kind = 2 if pool is left_pool else 3
        place = rows_of(pool, left_tile(way, d, far) + core, at, size)
        src = own.at[pl.ds(at, size)] if d == 0 and not far else place
        send(remote(src, place, came.at[0], row, core_col, kind), size, kind)

    def c_wait(pool, came):
        place = pool.at[pl.ds(0, 8 * ROWS)]
        remote(place, place, came.at[0], row, core_col, 2).wait_recv()

    def far_whole(incoming):
        place = rows_of(left_pool, left_tile(0, 0, incoming) + core, 0, ROWS)
        src = place if incoming else core_hbm
        return remote(src, place, far_came.at[0], row, far_col, 1), ROWS, 1

    def x_whole(way, d, far, incoming):
        tile = left_tile(way, d if incoming else d - 1, far) + core
        at, size = (0, ROWS) if d == 1 else (way * (ROWS // 2), ROWS // 2)
        place = rows_of(left_pool, tile, at, size)
        src = core_hbm if d == 1 and not far and not incoming else place
        return remote(src, place, x_came.at[way, d - 1, far], row, x_cols[way], 1), size, 1

    def x_take(d, far):
        for way in range(2):
            x_whole(way, d, far, True)[0].wait_recv()
            if d == 1:
                send(*x_whole(way, 2, far, False))
            at, size = (0, ROWS) if d == 1 else (way * (ROWS // 2), ROWS // 2)
            c_send(core_hbm, left_pool, c_came, way, d, far, at, size)

    def band_copy(owner, to, came):
        return pltpu.make_async_remote_copy(
            src_ref=message if came or owner is col else bands.at[owner],
            dst_ref=bands.at[owner],
            send_sem=sent.at[4],
            recv_sem=b_came.at[came],
            device_id=to,
            device_id_type=MESH,
        )

    send(*y_copy(0, 0, 0, False))
    for way in range(2):
        send(*z_copy(way, 1, OWN_LATE, False))
    for copy in local[:2]:
        copy.wait()

    support = vector_ref.shape[1]
    on_diagonal = iota((support, support), 0) == iota((support, support), 1)
    block_of = jnp.sum(jnp.where(on_diagonal, block_ref[...], 0), axis=1, keepdims=True)
    message[0] = vector_ref[0]
    message[1] = jnp.broadcast_to(block_of.astype(jnp.float32), (support, BS))

    band_copy(col, (row, far_col), 1).start()
    for way in range(2):
        send(*x_whole(way, 1, 0, False))
    for way in range(2):
        send(*z_copy(way, 1, OWN_EARLY, False))
    send(*far_whole(False))

    for partner in plane:
        band_copy(col, partner, 0).start()
    send(*y_copy(0, 0, 1, False))
    c_send(core_hbm, left_pool, c_came, 0, 0, 0, 0, ROWS)
    bands[col] = message[...]
    kept_ref[...] = message[...]
    local[2].wait()
    local[3].wait()

    unit = ones_where(iota((64, 64), 0) == iota((64, 64), 1))
    coords = lax.dot_general(
        unit,
        coords_ref[...].astype(jnp.float32),
        (((1,), (1,)), ((), ())),
        preferred_element_type=jnp.float32,
    )
    number, codes = products_here(coords, row, col)

    y_copy(0, 0, 0, True)[0].wait_recv()
    for way in range(2):
        send(*z_copy(way, 1, FAR_EARLY, False))

    at_line, at_lane = iota((64, 32), 0), iota((64, 32), 1)

    def coordinate(s, which):
        mask = (at_line == row * SLOTS + s) & (at_lane == col * 2 + which)
        return jnp.sum(jnp.where(mask, coords, 0.0))

    def vectors_on(block):
        return jnp.sum(jnp.where(bands[:, 1] == block, bands[:, 0], 0.0), axis=1)

    def all_bands(count):
        many = bands.at[pl.ds(0, count)]
        return pltpu.make_async_remote_copy(
            src_ref=many,
            dst_ref=many,
            send_sem=sent.at[4],
            recv_sem=b_came.at[0],
            device_id=(row, core_col),
            device_id_type=MESH,
        )

    row_base, col_base = (row * TILE).astype(jnp.float32), (col * TILE).astype(jnp.float32)

    def block_rows(at):
        return pl.ds(at * BS, BS)

    left_at = [(c >> 4) & 63 for c in codes]
    right_at = [((c >> 6) & 15) * SLOTS + ((c >> 2) & 3) for c in codes]
    target_at = [c & 3 for c in codes]
    middle = [((c >> 6) & 15) * TILE + (c >> 10) for c in codes]

    def middles(first, last):
        for t in range(min(first, ROOM), min(last, ROOM)):
            mid_vec[t] = vectors_on(middle[t].astype(jnp.float32))

    def right_terms(first, last):
        for t in range(min(first, ROOM), min(last, ROOM)):
            right_used[t] = outer(mid_vec[t], col_vec[target_at[t]])

    inverse = 1.0 / jnp.full((1, BS), spread[0], jnp.float32)
    scale = inverse * inverse

    def left_terms(first, last):
        for t in range(min(first, ROOM), min(last, ROOM)):
            exchange = outer(row_vec[target_at[t]], mid_vec[t])
            high, low = halves((left_pool[block_rows(left_at[t])] - exchange) * scale)
            left_high[t], left_low[t] = high, low

    z_take(1, OWN_LATE)
    band_copy(far_col, (row, far_col), 1).wait_recv()
    for partner in plane:
        band_copy(far_col, partner, 0).start()
    z_take(1, OWN_EARLY)
    x_take(1, 0)
    z_take(1, FAR_EARLY)
    x_take(2, 0)
    z_take(2, OWN_LATE)
    all_bands(14).wait_recv()
    for s in range(SLOTS):
        row_vec[s] = vectors_on(row_base + coordinate(s, 0))
        col_vec[s] = vectors_on(col_base + coordinate(s, 1))
    far_whole(True)[0].wait_recv()
    for way in range(2):
        send(*x_whole(way, 1, 1, False))
    c_send(core_hbm, left_pool, c_came, 0, 0, 1, 0, ROWS)
    middles(0, 10)
    z_take(2, OWN_EARLY)
    middles(10, ROOM)
    for copy in local[4:]:
        copy.wait()
    for s in range(SLOTS):
        fock[block_rows(s)] -= outer(row_vec[s], col_vec[s])
    z_take(2, FAR_EARLY)
    right_terms(0, 10)
    z_take(3, OWN_LATE)
    right_terms(10, ROOM)
    x_take(1, 1)
    z_take(3, OWN_EARLY)
    fits_here[0] = jnp.where(most_products(coords) <= ROOM, 1, 0).astype(jnp.int32)
    def weight(t, s):
        live = (number > float(t)) & (target_at[t] == s)
        return jnp.where(live, 1.0, 0.0).astype(jnp.float32)

    weights = [[weight(t, s) for s in range(SLOTS)] for t in range(ROOM)]

    flag = pltpu.make_async_copy(fits_here, fits_ref, came.at[7])
    flag.start()
    z_take(3, FAR_EARLY)
    x_take(2, 1)
    z_take(4, OWN_LATE)
    c_wait(left_pool, c_came)
    left_terms(0, 10)
    z_take(4, OWN_EARLY)
    left_terms(10, ROOM)
    z_take(4, FAR_EARLY)
    y_copy(0, 0, 1, True)[0].wait_recv()
    for d in range(1, 5):
        for way in range(2):
            y_copy(way, d, 1, True)[0].wait_recv()

    def weighted(s):
        total = left_used[0] * weights[0][s]
        for t in range(1, ROOM):
            total = total + left_used[t] * weights[t][s]
        return total

    for t in range(ROOM):
        high, low = halves(right_pool[block_rows(right_at[t])] - right_used[t])
        right_high[t], right_low[t] = high, low
        left_used[t] = product(left_high[t], left_low[t], high, low)
    for s in range(SLOTS):
        square[block_rows(s)] = weighted(s)

    def far_copy(way, d, late, incoming):
        at, size = span(late, EARLY_SQUARE, way, d == 2)
        tile = left_tile(way, d, incoming) + core
        place = rows_of(square_pool, tile, at, size)
        src = square.at[pl.ds(at, size)] if d == 0 and not incoming else place
        came = far2_came.at[way, d] if d else far2_came.at[late, 0]
        return remote(src, place, came, row, far_col, 3), size, 3

    def x_copy(way, d, item, incoming):
        late, far = item
        at, size = span(late, EARLY_SQUARE, way, d == 2)
        tile = left_tile(way, d if incoming else d - 1, far) + core
        place = rows_of(square_pool, tile, at, size)
        own = d == 1 and not far and not incoming
        src = square.at[pl.ds(at, size)] if own else place
        came = x2_came.at[way, d - 1, ITEMS.index(item)]
        return remote(src, place, came, row, x_cols[way], 3), size, 3

    def x2_take(d, item):
        late, far = item
        for way in range(2):
            x_copy(way, d, item, True)[0].wait_recv()
            if d == 1:
                send(*x_copy(way, 2, item, False))
            if item == OWN_LATE:
                send(*far_copy(way, d, 1, False))
            c_send(square, square_pool, c2_came, way, d, far, *span(late, EARLY_SQUARE, way, d == 2))

    def far2_take(way, d, late):
        far_copy(way, d, late, True)[0].wait_recv()
        at, size = span(late, EARLY_SQUARE, way, d == 2)
        c_send(square, square_pool, c2_came, way, d, 1, at, size)

    send(*far_copy(0, 0, 0, False))
    for way in range(2):
        send(*x_copy(way, 1, OWN_LATE, False))
    send(*far_copy(0, 0, 1, False))
    for way in range(2):
        send(*x_copy(way, 1, OWN_EARLY, False))
    c_send(square, square_pool, c2_came, 0, 0, 0, 0, ROWS)
    square_pool[tile_cols] = square[...]
    x2_take(1, OWN_LATE)
    far2_take(0, 0, 0)
    for way in range(2):
        send(*x_copy(way, 1, FAR_EARLY, False))
    x2_take(1, OWN_EARLY)
    x2_take(2, OWN_LATE)
    far2_take(0, 0, 1)
    x2_take(1, FAR_EARLY)
    x2_take(2, OWN_EARLY)
    far2_take(0, 1, 1)
    far2_take(1, 1, 1)
    x2_take(2, FAR_EARLY)
    far2_take(0, 2, 1)
    far2_take(1, 2, 1)
    c_wait(square_pool, c2_came)

    for t in range(ROOM):
        high, low = halves(square_pool[block_rows(left_at[t])])
        left_used[t] = product(high, low, right_high[t], right_low[t])
    for s in range(SLOTS):
        out_ref[s] = 1.5 * fock[block_rows(s)] - 2.0 * weighted(s)

    flag.wait()
    all_bands(15).wait_send()
    for kind, rows in enumerate(rows_sent):
        place = right_pool.at[pl.ds(0, rows)]
        remote(place, place, far_came.at[0], row, core_col, kind).wait_send()


def sparse(core_blocks, block_coords, band_vectors, band_blocks, spread):
    support = band_vectors.shape[1]
    f32 = jnp.float32
    block = (BS, BS)
    smem = pl.BlockSpec(memory_space=pltpu.SMEM)
    hbm = pl.BlockSpec(memory_space=pltpu.HBM)
    vmem = pl.BlockSpec(memory_space=pltpu.VMEM)
    dma = pltpu.SemaphoreType.DMA
    return pl.pallas_call(
        kernel,
        out_shape=(
            jax.ShapeDtypeStruct(core_blocks.shape, f32),
            jax.ShapeDtypeStruct((1,), jnp.int32),
            jax.ShapeDtypeStruct((2, support, BS), f32),
        ),
        in_specs=[hbm] * 5,
        out_specs=(vmem, hbm, vmem),
        scratch_shapes=[
            pltpu.SMEM((1,), f32),
            pltpu.VMEM(block_coords.shape[::-1], jnp.int32),
            pltpu.VMEM(band_vectors.shape, f32),
            pltpu.VMEM(band_blocks.shape, jnp.int32),
            dma((8,)),
            pltpu.SMEM((1,), jnp.int32),
            pltpu.VMEM((2, support, BS), f32),
            pltpu.VMEM((16, 2, support, BS), f32),
            pltpu.VMEM((16 * ROWS, BS), f32),
            pltpu.VMEM((16 * ROWS, BS), f32),
            pltpu.VMEM((16 * ROWS, BS), f32),
            pltpu.VMEM((ROWS, BS), f32),
            pltpu.VMEM((ROWS, BS), f32),
            pltpu.VMEM((SLOTS, 16, BS), f32),
            pltpu.VMEM((SLOTS, 16, BS), f32),
            pltpu.VMEM((ROOM, 16, BS), f32),
            pltpu.VMEM((ROOM, *block), f32),
            pltpu.VMEM((ROOM, *block), f32),
            pltpu.VMEM((ROOM, *block), jnp.bfloat16),
            pltpu.VMEM((ROOM, *block), jnp.bfloat16),
            pltpu.VMEM((ROOM, *block), jnp.bfloat16),
            pltpu.VMEM((ROOM, *block), jnp.bfloat16),
            dma((5,)),
            dma((2, 4, 3)),
            dma((2, 5)),
            dma((1,)),
            dma((2, 2, 2)),
            dma((1,)),
            dma((2,)),
            dma((2, 3)),
            dma((2, 2, 3)),
            dma((1,)),
        ],
        compiler_params=pltpu.CompilerParams(
            collective_id=0, has_side_effects=True
        ),
        name="sparse",
    )(spread.reshape(1), block_coords.T, core_blocks.reshape(ROWS, BS), band_vectors, band_blocks)


def on_device(core_blocks, block_coords, band_vectors, band_blocks, spread):
    purified, fits, band = sparse(core_blocks, block_coords, band_vectors, band_blocks, spread)

    def any_pattern():
        blocks = band[1:, :, 0].astype(jnp.int32)
        return general(core_blocks, block_coords, band[:1], blocks, spread)

    return lax.switch(fits[0], [any_pattern, lambda: purified])


def solution(mesh):
    placed = (P("row", "col", None), P(), P("col", None, None), P("col", None), P())
    return jax.shard_map(
        on_device, mesh=mesh, in_specs=placed, out_specs=P("row", "col", None), check_vma=False
    )
```

```python
import functools

import jax
import jax.numpy as jnp
from jax import lax
from jax.experimental import pallas as pl
from jax.experimental.pallas import tpu as pltpu
from jax.sharding import PartitionSpec as P

NB = 160
BS = 128
SLOTS = 4
MESH = pl.DeviceIdType.MESH

NZ = 8
NX = 4
TILE = 10
ROOM = 20
PAD = 256
ROWS = SLOTS * BS
EARLY = 256
EARLY_SQUARE = 272

highest = lax.Precision.HIGHEST


def shifted(block, axis, distance):
    devices = range(lax.axis_size(axis))
    route = [((i - distance) % len(devices), i) for i in devices]
    return lax.ppermute(block, axis, route)


def exchange_term(vectors, blocks, block_rows, block_cols):
    hit_row = (blocks[:, :, None] == block_rows[None, None, :]).astype(jnp.float32)
    hit_col = (blocks[:, :, None] == block_cols[None, None, :]).astype(jnp.float32)
    vec_row = jnp.einsum("bln,blx->bnx", hit_row, vectors, precision=highest)
    vec_col = jnp.einsum("bln,blx->bnx", hit_col, vectors, precision=highest)
    return -jnp.einsum("bnx,bny->nxy", vec_row, vec_col, precision=highest)


def tile_layout(layout, tile_row, tile_col):
    slots = layout.shape[1]
    start = (tile_row, jnp.int32(0), tile_col, jnp.int32(0))
    return lax.dynamic_slice(layout, start, (1, slots, 1, 2)).reshape(slots, 2)


def link_weights(targets, left_local, piece, right_local, tile_rows):
    row_target = targets[:, None, None, 0]
    col_target = targets[:, None, None, 1]
    row_left = left_local[None, :, None, 0]
    col_left = left_local[None, :, None, 1]
    row_right = right_local[None, None, :, 0]
    col_right = right_local[None, None, :, 1]
    keep = (row_left == row_target) & (col_left // tile_rows == piece)
    keep = keep & (col_left % tile_rows == row_right) & (col_right == col_target)
    return keep.astype(jnp.float32)


def accumulate(
    total, targets, left_blocks, left_local, piece, right_blocks, right_local, tile_rows
):
    weight = link_weights(targets, left_local, piece, right_local, tile_rows)
    pairs = jnp.einsum("axk,bky->axby", left_blocks, right_blocks, precision=highest)
    return total + jnp.einsum("tab,axby->txy", weight, pairs, precision=highest)


def align(block, axis, amount):
    for place in range((lax.axis_size(axis) - 1).bit_length()):
        moved = shifted(block, axis, -(1 << place))
        block = jnp.where(amount >> place & 1 == 1, moved, block)
    return block


def shifted_product(left, right, layout, targets, this_row, this_col, tile_rows):
    row_count = lax.axis_size("row")
    left = align(left, "col", this_row)

    def step_body(step, carry):
        total, left, right = carry
        source = (this_row + this_col + step) % row_count
        left_local = tile_layout(layout, this_row, source)
        right_local = tile_layout(layout, source, this_col)
        total = accumulate(
            total, targets, left, left_local, 0, right, right_local, tile_rows
        )
        left = shifted(left, "col", -1)
        right = shifted(right, "row", -1)
        return (total, left, right)

    total, left, right = lax.fori_loop(
        0, row_count, step_body, (jnp.zeros_like(left), left, right)
    )
    return (total, right)


def general(core_blocks, block_coords, band_vectors, band_blocks, spread):
    row_count = lax.axis_size("row")
    column_count = lax.axis_size("col")
    tile_rows = NB // row_count
    tile_columns = NB // column_count
    slots = core_blocks.shape[0]
    this_row = lax.axis_index("row")
    this_col = lax.axis_index("col")
    layout = block_coords.reshape(row_count, slots, column_count, 2)
    targets = tile_layout(layout, this_row, this_col)
    vectors, blocks = (
        lax.all_gather(band_vectors, "col", axis=0, tiled=True),
        lax.all_gather(band_blocks, "col", axis=0, tiled=True),
    )
    block_rows = this_row * tile_rows + targets[:, 0]
    block_cols = this_col * tile_columns + targets[:, 1]
    exchange = exchange_term(vectors, blocks, block_rows, block_cols)
    fock = core_blocks + exchange
    scaled = fock / spread
    right = align(scaled, "row", this_col)
    square, right = shifted_product(
        scaled, right, layout, targets, this_row, this_col, tile_rows
    )
    cube, right = shifted_product(
        square, right, layout, targets, this_row, this_col, tile_rows
    )
    return 1.5 * fock - 2.0 * spread * cube


def iota(shape, axis):
    return lax.broadcasted_iota(jnp.int32, shape, axis)


def ones_where(mask):
    return jnp.where(mask, 1.0, 0.0).astype(jnp.float32)


def times(left, right, precision=None):
    return jnp.dot(left, right, precision=precision, preferred_element_type=jnp.float32)


def halves(block):
    high = block.astype(jnp.bfloat16)
    return high, (block - high.astype(jnp.float32)).astype(jnp.bfloat16)


def product(left_high, left_low, right_high, right_low):
    total = times(left_high, right_low) + times(left_low, right_high)
    return total + times(left_high, right_high)


def outer(left, right):
    return lax.dot_general(
        left,
        right,
        (((0,), (0,)), ((), ())),
        precision=highest,
        preferred_element_type=jnp.float32,
    )


def most_products(coords):
    i, c = iota((PAD, 16), 0), iota((PAD, 16), 1)
    down = (i >= c * TILE) & (i < c * TILE + TILE)
    row_at = jnp.sum(jnp.where(down, i - c * TILE + 1, 0), axis=1, keepdims=True) - 1
    r, j = iota((16, PAD), 0), iota((16, PAD), 1)
    along = (j >= r * TILE) & (j < r * TILE + TILE)
    col_at = jnp.sum(jnp.where(along, j - r * TILE + 1, 0), axis=0, keepdims=True) - 1
    row_at, col_at = row_at.astype(jnp.float32), col_at.astype(jnp.float32)
    down, along = ones_where(down), ones_where(along)
    line, tile = iota((32, 16), 0), iota((32, 16), 1)
    rows = times(coords, ones_where(line == 2 * tile))
    cols = times(coords, ones_where(line == 2 * tile + 1))
    pattern = jnp.zeros((PAD, PAD), jnp.float32)
    for s in range(SLOTS):
        of_slot = ones_where(iota((16, 64), 1) == iota((16, 64), 0) * SLOTS + s)
        q = times(times(down, times(of_slot, rows)), along)
        p = times(times(down, times(of_slot, cols)), along)
        pattern = jnp.where((q == row_at) & (p == col_at), 1.0, pattern)
    links = pattern * times(pattern, pattern)
    return jnp.max(times(times(along, links), down))


def products_here(coords, row, col):
    line, lane = iota((64, 32), 0), iota((64, 32), 1)
    high, wide = iota((64, 64), 0), iota((64, 64), 1)
    i, pair = iota((64, 16), 0), iota((64, 16), 1)

    def at_lane(array, place):
        return jnp.sum(jnp.where(lane == place, array, 0.0), axis=1, keepdims=True)

    strip = times(ones_where(wide == row * SLOTS + (high & 3)), coords)
    left_row = at_lane(strip, (line >> 2) * 2)
    left_col = at_lane(strip, (line >> 2) * 2 + 1)
    here_row, here_col = at_lane(coords, col * 2), at_lane(coords, col * 2 + 1)
    same_tile = ones_where((high >> 2) == (wide >> 2))
    of_right = (i & 3) == (pair >> 2)
    right_row = times(same_tile, jnp.where(of_right, here_row, 0.0))
    right_col = times(same_tile, jnp.where(of_right, here_col, 0.0))
    of_target = i == row * SLOTS + (pair & 3)
    everywhere = jnp.ones((64, 64), jnp.float32)
    target_row = times(everywhere, jnp.where(of_target, here_row, 0.0))
    target_col = times(everywhere, jnp.where(of_target, here_col, 0.0))
    hit = (left_row == target_row) & (left_col == right_row) & (right_col == target_col)
    found = ones_where(hit)
    in_line = jnp.broadcast_to(jnp.sum(found, axis=1, keepdims=True), (64, 16))
    before = ones_where(iota((16, 16), 0) < iota((16, 16), 1))
    rank = times(ones_where(wide < high), in_line) + times(found, before)
    rank = jnp.where(hit, rank, -1.0)
    code = (i * 16 + pair).astype(jnp.float32) + 1024.0 * left_col
    number = jnp.sum(found)
    codes = [jnp.sum(jnp.where(rank == float(t), code, 0.0)) for t in range(ROOM)]
    return number, [c.astype(jnp.int32) for c in codes]


def kernel(
    spread_hbm,
    coords_hbm,
    core_hbm,
    vector_hbm,
    block_hbm,
    out_ref,
    fits_ref,
    kept_ref,
    spread,
    coords_ref,
    vector_ref,
    block_ref,
    came,
    fits_here,
    message,
    bands,
    right_pool,
    left_pool,
    square_pool,
    fock,
    square,
    row_vec,
    col_vec,
    mid_vec,
    left_used,
    right_used,
    left_high,
    left_low,
    right_high,
    right_low,
    sent,
    z_came,
    y_came,
    far_came,
    x_came,
    c_came,
    b_came,
    far2_came,
    x2_came,
    c2_came,
):
    row = lax.axis_index("row")
    col = lax.axis_index("col")
    z, y_lo = row // 2, row % 2
    y_hi, x, core = col // 8, col // 2 % NX, col % 2
    z_rows = ((row + 2) % 16, (row + 14) % 16)
    y_row = row + 1 - 2 * y_lo
    base = col - x * 2
    x_cols = (base + (x + 1) % NX * 2, base + (x + NX - 1) % NX * 2)
    core_col = col + 1 - 2 * core
    far_col = (col + 8) % 16
    plane = [(row, y_hi * 8 + (col + step) % 8) for step in range(1, 8)]

    gate = pltpu.get_barrier_semaphore()
    greet = [(z_rows[0], col), (z_rows[1], col), (y_row, col)]
    greet += [(row, far_col)] + plane
    for partner in greet:
        pl.semaphore_signal(gate, inc=1, device_id=partner, device_id_type=MESH)

    tile_rows = pl.ds(pl.multiple_of(row * ROWS, ROWS), ROWS)
    tile_cols = pl.ds(pl.multiple_of(col * ROWS, ROWS), ROWS)
    local = [
        pltpu.make_async_copy(vector_hbm, vector_ref, came.at[0]),
        pltpu.make_async_copy(block_hbm, block_ref, came.at[1]),
        pltpu.make_async_copy(coords_hbm, coords_ref, came.at[2]),
        pltpu.make_async_copy(spread_hbm, spread, came.at[3]),
        pltpu.make_async_copy(core_hbm, right_pool.at[tile_rows], came.at[4]),
        pltpu.make_async_copy(core_hbm, left_pool.at[tile_cols], came.at[5]),
        pltpu.make_async_copy(core_hbm, fock, came.at[6]),
    ]
    for copy in local:
        copy.start()
    pl.semaphore_wait(gate, len(greet))

    rows_sent = [0, 0, 0, 0]

    def remote(src, dst, came, to_row, to_col, kind):
        return pltpu.make_async_remote_copy(
            src_ref=src,
            dst_ref=dst,
            send_sem=sent.at[kind],
            recv_sem=came,
            device_id=(to_row, to_col),
            device_id_type=MESH,
        )

    def send(copy, rows, kind):
        copy.start()
        rows_sent[kind] += rows

    OWN_LATE, OWN_EARLY, FAR_EARLY = (1, 0), (0, 0), (0, 1)
    ITEMS = (OWN_LATE, OWN_EARLY, FAR_EARLY)

    def turned(at, size, way, distance):
        return (at + (size - distance if way == 0 else distance)) % size

    def span(late, early, way, last):
        at, size = (early, ROWS - early) if late else (0, early)
        return (at + way * (size // 2), size // 2) if last else (at, size)

    def rows_of(pool, tile, at, size):
        return pool.at[pl.ds(pl.multiple_of(tile * ROWS + at, 8), size)]

    def z_copy(way, d, item, incoming):
        late, far = item
        tile = turned(z, NZ, way, d if incoming else d - 1)
        plane = 1 - y_lo if far else y_lo
        at, size = span(late, EARLY, way, d == 4)
        place = rows_of(right_pool, tile * 2 + plane, at, size)
        own = d == 1 and not far and not incoming
        src = core_hbm.at[pl.ds(at, size)] if own else place
        came = z_came.at[way, d - 1, ITEMS.index(item)]
        return remote(src, place, came, z_rows[way], col, 0), size, 0

    def y_copy(way, d, late, incoming):
        tile = z if d == 0 else turned(z, NZ, way, d)
        plane = 1 - y_lo if incoming else y_lo
        at, size = span(late, EARLY, way, d == 4)
        place = rows_of(right_pool, tile * 2 + plane, at, size)
        src = core_hbm.at[pl.ds(at, size)] if d == 0 and not incoming else place
        came = y_came.at[way, d] if d else y_came.at[late, 0]
        return remote(src, place, came, y_row, col, 1), size, 1

    def z_take(d, item):
        for way in range(2):
            z_copy(way, d, item, True)[0].wait_recv()
            if d < 4:
                send(*z_copy(way, d + 1, item, False))
            if item == OWN_LATE:
                send(*y_copy(way, d, 1, False))

    def left_tile(way, d, far):
        return ((1 - y_hi if far else y_hi) * 8) + turned(x, NX, way, d) * 2

    def c_send(own, pool, came, way, d, far, at, size):
        kind = 2 if pool is left_pool else 3
        place = rows_of(pool, left_tile(way, d, far) + core, at, size)
        src = own.at[pl.ds(at, size)] if d == 0 and not far else place
        send(remote(src, place, came.at[0], row, core_col, kind), size, kind)

    def c_wait(pool, came):
        place = pool.at[pl.ds(0, 8 * ROWS)]
        remote(place, place, came.at[0], row, core_col, 2).wait_recv()

    def far_whole(incoming):
        place = rows_of(left_pool, left_tile(0, 0, incoming) + core, 0, ROWS)
        src = place if incoming else core_hbm
        return remote(src, place, far_came.at[0], row, far_col, 1), ROWS, 1

    def x_whole(way, d, far, incoming):
        tile = left_tile(way, d if incoming else d - 1, far) + core
        at, size = (0, ROWS) if d == 1 else (way * (ROWS // 2), ROWS // 2)
        place = rows_of(left_pool, tile, at, size)
        src = core_hbm if d == 1 and not far and not incoming else place
        return remote(src, place, x_came.at[way, d - 1, far], row, x_cols[way], 1), size, 1

    def x_take(d, far):
        for way in range(2):
            x_whole(way, d, far, True)[0].wait_recv()
            if d == 1:
                send(*x_whole(way, 2, far, False))
            at, size = (0, ROWS) if d == 1 else (way * (ROWS // 2), ROWS // 2)
            c_send(core_hbm, left_pool, c_came, way, d, far, at, size)

    def band_copy(owner, to, came):
        return pltpu.make_async_remote_copy(
            src_ref=message if came or owner is col else bands.at[owner],
            dst_ref=bands.at[owner],
            send_sem=sent.at[4],
            recv_sem=b_came.at[came],
            device_id=to,
            device_id_type=MESH,
        )

    send(*y_copy(0, 0, 0, False))
    for way in range(2):
        send(*z_copy(way, 1, OWN_LATE, False))
    for copy in local[:2]:
        copy.wait()

    support = vector_ref.shape[1]
    on_diagonal = iota((support, support), 0) == iota((support, support), 1)
    block_of = jnp.sum(jnp.where(on_diagonal, block_ref[...], 0), axis=1, keepdims=True)
    message[0] = vector_ref[0]
    message[1] = jnp.broadcast_to(block_of.astype(jnp.float32), (support, BS))

    band_copy(col, (row, far_col), 1).start()
    for way in range(2):
        send(*x_whole(way, 1, 0, False))
    for way in range(2):
        send(*z_copy(way, 1, OWN_EARLY, False))
    send(*far_whole(False))

    for partner in plane:
        band_copy(col, partner, 0).start()
    send(*y_copy(0, 0, 1, False))
    c_send(core_hbm, left_pool, c_came, 0, 0, 0, 0, ROWS)
    bands[col] = message[...]
    kept_ref[...] = message[...]
    local[2].wait()
    local[3].wait()

    unit = ones_where(iota((64, 64), 0) == iota((64, 64), 1))
    coords = lax.dot_general(
        unit,
        coords_ref[...].astype(jnp.float32),
        (((1,), (1,)), ((), ())),
        preferred_element_type=jnp.float32,
    )
    number, codes = products_here(coords, row, col)

    y_copy(0, 0, 0, True)[0].wait_recv()
    for way in range(2):
        send(*z_copy(way, 1, FAR_EARLY, False))

    at_line, at_lane = iota((64, 32), 0), iota((64, 32), 1)

    def coordinate(s, which):
        mask = (at_line == row * SLOTS + s) & (at_lane == col * 2 + which)
        return jnp.sum(jnp.where(mask, coords, 0.0))

    def vectors_on(block):
        return jnp.sum(jnp.where(bands[:, 1] == block, bands[:, 0], 0.0), axis=1)

    def all_bands(count):
        many = bands.at[pl.ds(0, count)]
        return pltpu.make_async_remote_copy(
            src_ref=many,
            dst_ref=many,
            send_sem=sent.at[4],
            recv_sem=b_came.at[0],
            device_id=(row, core_col),
            device_id_type=MESH,
        )

    row_base, col_base = (row * TILE).astype(jnp.float32), (col * TILE).astype(jnp.float32)

    def block_rows(at):
        return pl.ds(at * BS, BS)

    left_at = [(c >> 4) & 63 for c in codes]
    right_at = [((c >> 6) & 15) * SLOTS + ((c >> 2) & 3) for c in codes]
    target_at = [c & 3 for c in codes]
    middle = [((c >> 6) & 15) * TILE + (c >> 10) for c in codes]

    def middles(first, last):
        for t in range(min(first, ROOM), min(last, ROOM)):
            mid_vec[t] = vectors_on(middle[t].astype(jnp.float32))

    def right_terms(first, last):
        for t in range(min(first, ROOM), min(last, ROOM)):
            right_used[t] = outer(mid_vec[t], col_vec[target_at[t]])

    inverse = 1.0 / jnp.full((1, BS), spread[0], jnp.float32)
    scale = inverse * inverse

    def left_terms(first, last):
        for t in range(min(first, ROOM), min(last, ROOM)):
            exchange = outer(row_vec[target_at[t]], mid_vec[t])
            high, low = halves((left_pool[block_rows(left_at[t])] - exchange) * scale)
            left_high[t], left_low[t] = high, low

    z_take(1, OWN_LATE)
    band_copy(far_col, (row, far_col), 1).wait_recv()
    for partner in plane:
        band_copy(far_col, partner, 0).start()
    z_take(1, OWN_EARLY)
    x_take(1, 0)
    z_take(1, FAR_EARLY)
    x_take(2, 0)
    z_take(2, OWN_LATE)
    all_bands(14).wait_recv()
    for s in range(SLOTS):
        row_vec[s] = vectors_on(row_base + coordinate(s, 0))
        col_vec[s] = vectors_on(col_base + coordinate(s, 1))
    far_whole(True)[0].wait_recv()
    for way in range(2):
        send(*x_whole(way, 1, 1, False))
    c_send(core_hbm, left_pool, c_came, 0, 0, 1, 0, ROWS)
    middles(0, 10)
    z_take(2, OWN_EARLY)
    middles(10, ROOM)
    for copy in local[4:]:
        copy.wait()
    for s in range(SLOTS):
        fock[block_rows(s)] -= outer(row_vec[s], col_vec[s])
    z_take(2, FAR_EARLY)
    right_terms(0, 10)
    z_take(3, OWN_LATE)
    right_terms(10, ROOM)
    x_take(1, 1)
    z_take(3, OWN_EARLY)
    fits_here[0] = jnp.where(most_products(coords) <= ROOM, 1, 0).astype(jnp.int32)
    def weight(t, s):
        live = (number > float(t)) & (target_at[t] == s)
        return jnp.where(live, 1.0, 0.0).astype(jnp.float32)

    weights = [[weight(t, s) for s in range(SLOTS)] for t in range(ROOM)]

    flag = pltpu.make_async_copy(fits_here, fits_ref, came.at[7])
    flag.start()
    z_take(3, FAR_EARLY)
    x_take(2, 1)
    z_take(4, OWN_LATE)
    c_wait(left_pool, c_came)
    left_terms(0, 10)
    z_take(4, OWN_EARLY)
    left_terms(10, ROOM)
    z_take(4, FAR_EARLY)
    y_copy(0, 0, 1, True)[0].wait_recv()
    for d in range(1, 5):
        for way in range(2):
            y_copy(way, d, 1, True)[0].wait_recv()

    def weighted(s):
        total = left_used[0] * weights[0][s]
        for t in range(1, ROOM):
            total = total + left_used[t] * weights[t][s]
        return total

    for t in range(ROOM):
        high, low = halves(right_pool[block_rows(right_at[t])] - right_used[t])
        right_high[t], right_low[t] = high, low
        left_used[t] = product(left_high[t], left_low[t], high, low)
    for s in range(SLOTS):
        square[block_rows(s)] = weighted(s)

    def far_copy(way, d, late, incoming):
        at, size = span(late, EARLY_SQUARE, way, d == 2)
        tile = left_tile(way, d, incoming) + core
        place = rows_of(square_pool, tile, at, size)
        src = square.at[pl.ds(at, size)] if d == 0 and not incoming else place
        came = far2_came.at[way, d] if d else far2_came.at[late, 0]
        return remote(src, place, came, row, far_col, 3), size, 3

    def x_copy(way, d, item, incoming):
        late, far = item
        at, size = span(late, EARLY_SQUARE, way, d == 2)
        tile = left_tile(way, d if incoming else d - 1, far) + core
        place = rows_of(square_pool, tile, at, size)
        own = d == 1 and not far and not incoming
        src = square.at[pl.ds(at, size)] if own else place
        came = x2_came.at[way, d - 1, ITEMS.index(item)]
        return remote(src, place, came, row, x_cols[way], 3), size, 3

    def x2_take(d, item):
        late, far = item
        for way in range(2):
            x_copy(way, d, item, True)[0].wait_recv()
            if d == 1:
                send(*x_copy(way, 2, item, False))
            if item == OWN_LATE:
                send(*far_copy(way, d, 1, False))
            c_send(square, square_pool, c2_came, way, d, far, *span(late, EARLY_SQUARE, way, d == 2))

    def far2_take(way, d, late):
        far_copy(way, d, late, True)[0].wait_recv()
        at, size = span(late, EARLY_SQUARE, way, d == 2)
        c_send(square, square_pool, c2_came, way, d, 1, at, size)

    send(*far_copy(0, 0, 0, False))
    for way in range(2):
        send(*x_copy(way, 1, OWN_LATE, False))
    send(*far_copy(0, 0, 1, False))
    for way in range(2):
        send(*x_copy(way, 1, OWN_EARLY, False))
    c_send(square, square_pool, c2_came, 0, 0, 0, 0, ROWS)
    square_pool[tile_cols] = square[...]
    x2_take(1, OWN_LATE)
    far2_take(0, 0, 0)
    for way in range(2):
        send(*x_copy(way, 1, FAR_EARLY, False))
    x2_take(1, OWN_EARLY)
    x2_take(2, OWN_LATE)
    far2_take(0, 0, 1)
    x2_take(1, FAR_EARLY)
    x2_take(2, OWN_EARLY)
    far2_take(0, 1, 1)
    far2_take(1, 1, 1)
    x2_take(2, FAR_EARLY)
    far2_take(0, 2, 1)
    far2_take(1, 2, 1)
    c_wait(square_pool, c2_came)

    for t in range(ROOM):
        high, low = halves(square_pool[block_rows(left_at[t])])
        left_used[t] = product(high, low, right_high[t], right_low[t])
    for s in range(SLOTS):
        out_ref[s] = 1.5 * fock[block_rows(s)] - 2.0 * weighted(s)

    flag.wait()
    all_bands(15).wait_send()
    for kind, rows in enumerate(rows_sent):
        place = right_pool.at[pl.ds(0, rows)]
        remote(place, place, far_came.at[0], row, core_col, kind).wait_send()


def sparse(core_blocks, block_coords, band_vectors, band_blocks, spread):
    support = band_vectors.shape[1]
    f32 = jnp.float32
    block = (BS, BS)
    smem = pl.BlockSpec(memory_space=pltpu.SMEM)
    hbm = pl.BlockSpec(memory_space=pltpu.HBM)
    vmem = pl.BlockSpec(memory_space=pltpu.VMEM)
    dma = pltpu.SemaphoreType.DMA
    return pl.pallas_call(
        kernel,
        out_shape=(
            jax.ShapeDtypeStruct(core_blocks.shape, f32),
            jax.ShapeDtypeStruct((1,), jnp.int32),
            jax.ShapeDtypeStruct((2, support, BS), f32),
        ),
        in_specs=[hbm] * 5,
        out_specs=(vmem, hbm, vmem),
        scratch_shapes=[
            pltpu.SMEM((1,), f32),
            pltpu.VMEM(block_coords.shape[::-1], jnp.int32),
            pltpu.VMEM(band_vectors.shape, f32),
            pltpu.VMEM(band_blocks.shape, jnp.int32),
            dma((8,)),
            pltpu.SMEM((1,), jnp.int32),
            pltpu.VMEM((2, support, BS), f32),
            pltpu.VMEM((16, 2, support, BS), f32),
            pltpu.VMEM((16 * ROWS, BS), f32),
            pltpu.VMEM((16 * ROWS, BS), f32),
            pltpu.VMEM((16 * ROWS, BS), f32),
            pltpu.VMEM((ROWS, BS), f32),
            pltpu.VMEM((ROWS, BS), f32),
            pltpu.VMEM((SLOTS, 16, BS), f32),
            pltpu.VMEM((SLOTS, 16, BS), f32),
            pltpu.VMEM((ROOM, 16, BS), f32),
            pltpu.VMEM((ROOM, *block), f32),
            pltpu.VMEM((ROOM, *block), f32),
            pltpu.VMEM((ROOM, *block), jnp.bfloat16),
            pltpu.VMEM((ROOM, *block), jnp.bfloat16),
            pltpu.VMEM((ROOM, *block), jnp.bfloat16),
            pltpu.VMEM((ROOM, *block), jnp.bfloat16),
            dma((5,)),
            dma((2, 4, 3)),
            dma((2, 5)),
            dma((1,)),
            dma((2, 2, 2)),
            dma((1,)),
            dma((2,)),
            dma((2, 3)),
            dma((2, 2, 3)),
            dma((1,)),
        ],
        compiler_params=pltpu.CompilerParams(
            collective_id=0, has_side_effects=True
        ),
        name="sparse",
    )(spread.reshape(1), block_coords.T, core_blocks.reshape(ROWS, BS), band_vectors, band_blocks)


def on_device(core_blocks, block_coords, band_vectors, band_blocks, spread):
    purified, fits, band = sparse(core_blocks, block_coords, band_vectors, band_blocks, spread)

    def any_pattern():
        blocks = band[1:, :, 0].astype(jnp.int32)
        return general(core_blocks, block_coords, band[:1], blocks, spread)

    return lax.switch(fits[0], [any_pattern, lambda: purified])


def solution(mesh):
    placed = (P("row", "col", None), P(), P("col", None, None), P("col", None), P())
    return jax.shard_map(
        on_device, mesh=mesh, in_specs=placed, out_specs=P("row", "col", None), check_vma=False
    )
```
